128 devices in a mesh: tm: 16 (over y_hi, z, core), sta: 8 (over y_lo, x).
Axes of the slice: x: 4, y: 4 (y_hi: 2, y_lo: 2; y = y_hi * 2 + y_lo), z: 4, core: 2. Of those that a mesh axis runs over, the one named last changes fastest.
Arguments:
- waveforms: bfloat16 [240, 8192], P('sta', 'tm'), may hold values from -6 to 6
- templates: bfloat16 [32, 64, 240, 100], P('tm', None, 'sta'), may hold values from -6 to 6
- available: int32 [32, 64, 240], P('tm', None, 'sta'), may hold values 0 or 1
- moveout: int32 [32, 64, 240], P('tm', None, 'sta'), may hold values from 0 to 63
- bank_blocks: int32 [2], replicated, may hold values from 0 to 31
Outputs:
- detect_sum: float32 [128, 8192], P('sta', 'tm')
The draws below stay inside these ranges and needn't reach their ends.
Inputs may be any that keep to these rules, and one draw needn't show every extreme that they name: `bank_blocks`: block b is stored at index b // 2 of tm.
All inputs are finite; a program needn't handle non-finite values. No bound on the sum of `available` on one device may be relied on, other than what follows from the above.
Results may differ from the reference program's by a relative error of at most 0.0029.
Values may be sent and summed in bfloat16 or wider, within the bound.
A program may use at most 128 MiB of HBM per device.

```python
import jax
import jax.numpy as jnp
from jax import lax

EVENTS = 64
TLEN = 100
MOVE = 64
CHANNELS = 240
TIME = 8192
BLOCKS = 32
TEMPLATES = 128


def set_ends(values, stream_key, smallest, largest):
    dims = values.shape
    spot = [jax.random.randint(jax.random.fold_in(stream_key, axis), (), 0, dims[axis]) for axis in range(len(dims))]
    values = values.at[tuple(spot)].set(smallest)
    longest = dims.index(max(dims))
    spot[longest] = (spot[longest] + 1) % dims[longest]
    return values.at[tuple(spot)].set(largest)


def shard_levels(key, dims, cuts, smallest, high):
    def one(position, parts):
        heights = jax.random.uniform(jax.random.fold_in(jax.random.fold_in(key, 6), position), (parts,), jnp.float32, smallest / len(cuts), high / len(cuts))
        return jnp.repeat(jnp.exp(heights), dims[position] // parts).reshape((-1,) + (1,) * (len(dims) - position - 1))

    factor_of = one(*cuts[0])
    for cut in cuts[1:]:
        factor_of = factor_of * one(*cut)
    return factor_of


def gaussian(own_key, extent, width, reach, shards=(), kind=jnp.bfloat16):
    drawn = width * jax.random.normal(own_key, extent, jnp.float32)
    if shards:
        drawn = drawn * shard_levels(own_key, extent, shards, -0.22, 0.18)
    return jnp.clip(drawn, -reach, reach).astype(kind)


def setup_inputs(seed: int = 0) -> dict:
    keys = jax.random.split(jax.random.key(seed), 6)
    return {
        "waveforms": gaussian(keys[0], (CHANNELS, TIME), 1.0, 6.0, ((0, 8), (1, 16))),
        "templates": gaussian(keys[1], (BLOCKS, EVENTS, CHANNELS, TLEN), 1.0, 6.0, ((0, 16), (2, 8))),
        "available": set_ends((jax.random.randint(keys[2], (BLOCKS, EVENTS, CHANNELS), 0, 4) < 3).astype(jnp.int32), jax.random.fold_in(keys[2], 1), 0, 1),
        "moveout": set_ends(jax.random.randint(keys[3], (BLOCKS, EVENTS, CHANNELS), 0, MOVE), jax.random.fold_in(keys[3], 1), 0, MOVE - 1).astype(jnp.int32),
        "bank_blocks": jax.random.randint(keys[4], (2,), 0, BLOCKS).astype(jnp.int32),
    }


epsilon = 1e-06
block_span = 512

def normalize_bank(bank):
    values = bank.astype(jnp.float32)
    center = lax.optimization_barrier(jnp.mean(values, axis=-1, keepdims=True))
    deviate = values - center
    spread = jnp.sqrt(lax.optimization_barrier(jnp.mean(deviate * deviate, axis=-1, keepdims=True)) + epsilon)
    return (deviate / (spread * bank.shape[-1])).astype(jnp.bfloat16)

def window_sigma(padded, length, tlen):
    first_sum = jnp.zeros((padded.shape[0], length), jnp.float32)
    second_sum = jnp.zeros((padded.shape[0], length), jnp.float32)
    for lag in range(tlen):
        piece = padded[:, lag:lag + length].astype(jnp.float32)
        first_sum = first_sum + piece
        second_sum = second_sum + piece * piece
    mean_value = first_sum / tlen
    return jnp.sqrt(second_sum / tlen - mean_value * mean_value + epsilon)

def reference(waveforms, templates, available, moveout, bank_blocks):
    tlen = templates.shape[3]
    total_len = waveforms.shape[1]
    chosen = templates[bank_blocks].reshape(TEMPLATES, CHANNELS, tlen)
    unit_norm_templates = normalize_bank(chosen).astype(jnp.float32)
    weights = available[bank_blocks].reshape(TEMPLATES, CHANNELS).astype(jnp.float32)
    shifts = moveout[bank_blocks].reshape(TEMPLATES, CHANNELS).astype(jnp.int32)
    padded = jnp.pad(waveforms, ((0, 0), (0, MOVE + tlen - 1)))
    sigma = window_sigma(padded, total_len + MOVE, tlen)

    def one_window(block):
        reference_sample = block * block_span
        segment = lax.dynamic_slice_in_dim(padded, reference_sample, block_span + MOVE + tlen - 1, 1)
        stacked_correlation = jnp.stack([segment[:, lag:lag + block_span + MOVE] for lag in range(tlen)], axis=1).astype(jnp.float32)
        correlation_values = jnp.einsum('ofn,fnw->ofw', unit_norm_templates, stacked_correlation)
        scaled_traces = correlation_values / lax.dynamic_slice_in_dim(sigma, reference_sample, block_span + MOVE, 1)[None]
        index_grid = jnp.arange(block_span, dtype=jnp.int32)[None, None, :] + shifts[:, :, None]
        picked = jnp.take_along_axis(scaled_traces, index_grid, axis=2)
        return lax.optimization_barrier(jnp.sum(picked * weights[:, :, None], axis=1))
    result = lax.map(one_window, jnp.arange(total_len // block_span, dtype=jnp.int32))
    return jnp.transpose(result, (1, 0, 2)).reshape(TEMPLATES, total_len)
```

```python
import jax
import jax.numpy as jnp
from jax import lax
from jax.experimental import pallas as pl
from jax.experimental.pallas import tpu as pltpu
from jax.sharding import PartitionSpec as P

TLEN = 100
MOVE = 64
EPS = 1e-06
SEG = 512
EXT = 768
CORR = 640
CH = 30
ROWS = 32
LANES = 128
HROWS = 112
MESH = pl.DeviceIdType.MESH
VMEM = pltpu.VMEM
MIB = 1 << 20


def place():
    tm = lax.axis_index("tm")
    return tm // 8, (tm // 2) % 4, tm % 2


def at_tm(y, z, h):
    return {"tm": y * 8 + z * 2 + h}


def remote(src, dst, send, recv, device):
    return pltpu.make_async_remote_copy(
        src_ref=src, dst_ref=dst, send_sem=send, recv_sem=recv, device_id=device, device_id_type=MESH
    )


def exchange_kernel(
    blocks, bank, wave, got_bank, got_wave, got_halo, cores, cand, pieces,
    local_sem, wave_send, wave_recv, halo_send, halo_recv, core_send, core_recv,
    piece_send, piece_recv, gather_send, gather_recv,
):
    y, z, h = place()
    barrier = pltpu.get_barrier_semaphore()
    tm = lax.axis_index("tm")
    own = pltpu.make_async_copy(bank.at[:, pl.ds(32 * h, 32)], cores.at[h], local_sem.at[0])
    own.start()
    own_wave = pltpu.make_async_copy(wave, got_wave.at[y, h], local_sem.at[1])
    own_wave.start()
    for d in range(1, 16):
        pl.semaphore_signal(barrier, inc=1, device_id={"tm": (tm + d) % 16}, device_id_type=MESH)
    pl.semaphore_wait(barrier, 15)

    to_core = remote(
        bank.at[:, pl.ds(32 * (1 - h), 32)], cores.at[h], core_send, core_recv, at_tm(y, z, 1 - h)
    )
    to_core.start()
    waves = []
    for dy, dh in ((0, 1), (1, 0), (1, 1)):
        i = dy * 2 + dh - 1
        copy = remote(
            wave, got_wave.at[y, h], wave_send.at[i], wave_recv.at[i],
            at_tm((y + dy) % 2, z, (h + dh) % 2),
        )
        copy.start()
        waves.append(copy)

    run = jnp.where(z > 0, y, 1 - y)

    def halo_copy(k):
        return remote(
            wave.at[:, pl.ds(0, 256)], got_halo.at[run], halo_send.at[k], halo_recv.at[run],
            at_tm(k // 2, (z + 3) % 4, k % 2),
        )

    @pl.when(h == 0)
    def _():
        for k in range(4):
            halo_copy(k).start()

    own.wait()
    to_core.wait()
    for q in range(2):
        b = blocks[q]
        cand[q] = cores[(b // 2) % 2, b % 2]

    sends = []
    for d in range(1, 8):
        y2, z2 = (y + d // 4) % 2, (z + d) % 4
        copy = remote(
            cand.at[y2, pl.ds(8 * z2, 8)], pieces.at[y, z], piece_send.at[d - 1], piece_recv.at[d - 1],
            at_tm(y2, z2, h),
        )
        copy.start()
        sends.append(copy)
    pieces[y, z] = cand[y, pl.ds(8 * z, 8)]
    for copy in sends:
        copy.wait()
    owner = blocks[y] // 2
    got_bank[z] = pieces[owner // 8, (owner // 2) % 4]
    gathers = []
    for d in range(1, 4):
        copy = remote(
            got_bank.at[z], got_bank.at[z], gather_send.at[d - 1], gather_recv.at[d - 1],
            at_tm(y, (z + d) % 4, h),
        )
        copy.start()
        gathers.append(copy)
    own_wave.wait()
    for copy in waves:
        copy.wait()
    for r in range(2):
        remote(
            wave.at[:, pl.ds(0, 256)], got_halo.at[r], halo_send.at[0], halo_recv.at[r], at_tm(0, (z + 1) % 4, 0)
        ).wait_recv()

    @pl.when(h == 0)
    def _():
        for k in range(4):
            halo_copy(k).wait_send()

    for copy in gathers:
        copy.wait()


def left(x, n):
    return pltpu.roll(x, x.shape[1] - n, 1)


def window_sum(x):
    two = x + left(x, 1)
    four = two + left(two, 2)
    eight = four + left(four, 4)
    sixteen = eight + left(eight, 8)
    half = sixteen + left(sixteen, 16)
    full = half + left(half, 32)
    return full + left(half, 64) + left(four, 96)


def correlate_kernel(bank, wave, halo, out, rows32, unit, index, ext, scale, hankel):
    y, z, h = place()
    lane = lax.broadcasted_iota(jnp.int32, (ROWS, LANES), 1)
    for s in range(4):
        run, core = s // 2, s % 2
        ext[s, 0:CH, 0:SEG] = wave[run, core].astype(jnp.float32)
        if core == 0:
            tail = wave[run, 1, :, 0:256].astype(jnp.float32)
        else:
            tail = halo[run].astype(jnp.float32)
            if run == 1:
                tail = jnp.where(z == 3, jnp.zeros_like(tail), tail)
        ext[s, 0:CH, SEG:EXT] = tail

    @pl.loop(0, 4)
    def _(s):
        x = ext[s]
        first = window_sum(x)[:, :CORR] * (1.0 / TLEN)
        second = window_sum(x * x)[:, :CORR] * (1.0 / TLEN)
        scale[s] = lax.rsqrt(second - first * first + EPS)

        @pl.loop(0, CH)
        def _(c):
            row = ext[s, pl.ds(c, 1), :]
            wide = jnp.broadcast_to(row, (HROWS, EXT))
            turned = pltpu.roll(wide, EXT - (HROWS - 1), 1, stride=1, stride_axis=0)
            hankel[s, c, 0:HROWS, :] = turned[:, :CORR].astype(jnp.bfloat16)
            hankel[s, c, HROWS:, :] = jnp.zeros((LANES - HROWS, CORR), jnp.bfloat16)

    lane8 = lax.broadcasted_iota(jnp.int32, (ROWS, LANES), 1)
    live = lane8 < TLEN

    @pl.loop(0, 32)
    def _(t):
        v = bank[t].astype(jnp.float32)
        v = jnp.where(live, v, 0.0)
        mean = jnp.sum(v, axis=1, keepdims=True) * (1.0 / TLEN)
        dev = jnp.where(live, v - mean, 0.0)
        spread = jnp.sqrt(jnp.sum(dev * dev, axis=1, keepdims=True) * (1.0 / TLEN) + EPS)
        u = dev / (spread * TLEN)
        sub = lax.broadcasted_iota(jnp.int32, (ROWS, LANES), 0)
        rows32[pl.ds(32 * t, 32), :] = jnp.where(sub < CH, u, v)

    avail = rows32[pl.ds(CH, 32, stride=32), :]
    shift = rows32[pl.ds(CH + 1, 32, stride=32), :]
    flip = (HROWS - 1 - lane) & (LANES - 1)
    for c in range(CH):
        u = rows32[pl.ds(c, 32, stride=32), :] * avail[:, c : c + 1]
        unit[c] = jnp.take_along_axis(u, flip, axis=1).astype(jnp.bfloat16)
        index[c] = lane + jnp.broadcast_to(shift[:, c : c + 1], (32, LANES)).astype(jnp.int32)

    for s in range(4):
        def channel(c, acc):
            corr = jnp.dot(unit[c], hankel[s, c], preferred_element_type=jnp.float32)
            corr = corr * scale[s, pl.ds(c, 1), :]
            where = index[c]
            inside = where < LANES
            at = where & (LANES - 1)
            turned = [
                jnp.take_along_axis(corr[:, LANES * m : LANES * (m + 1)], at, axis=1) for m in range(5)
            ]
            return tuple(a + jnp.where(inside, turned[m], turned[m + 1]) for m, a in enumerate(acc))

        acc = lax.fori_loop(
            0, CH, channel, tuple(jnp.zeros((32, LANES), jnp.float32) for _ in range(4)), unroll=5
        )
        for m in range(4):
            out[s, :, LANES * m : LANES * (m + 1)] = acc[m]


def reduce_kernel(part, out, got, send, recv):
    y, z, h = place()
    sta = lax.axis_index("sta")
    tm = lax.axis_index("tm")
    from_y, from_h = sta // 4, (sta // 2) % 2
    source_tm = from_y * 8 + z * 2 + from_h
    mine = source_tm == tm
    barrier = pltpu.get_barrier_semaphore()
    for s in range(8):
        @pl.when(jnp.logical_not(jnp.logical_and(mine, sta == s)))
        def _():
            pl.semaphore_signal(
                barrier, inc=1, device_id={"tm": source_tm, "sta": s}, device_id_type=MESH
            )

    @pl.when(mine)
    def _():
        pl.semaphore_wait(barrier, 7)

    @pl.when(jnp.logical_not(mine))
    def _():
        pl.semaphore_wait(barrier, 8)

    def copy(k):
        y2, h2, j = k // 4, (k // 2) % 2, k % 2
        to_tm = y2 * 8 + z * 2 + h2
        to_sta = 4 * y + 2 * h + j
        itself = jnp.logical_and(to_tm == tm, to_sta == sta)
        src = part.at[2 * y2 + h2, pl.ds(16 * j, 16)]
        return itself, src, remote(src, got.at[sta], send.at[k], recv.at[sta], {"tm": to_tm, "sta": to_sta})

    for k in range(8):
        itself, src, away = copy(k)

        @pl.when(jnp.logical_not(itself))
        def _():
            away.start()

        @pl.when(itself)
        def _():
            got[sta] = src[...]

    for k in range(8):
        itself, src, away = copy(k)

        @pl.when(jnp.logical_not(itself))
        def _():
            away.wait_send()

    for s in range(8):
        @pl.when(jnp.logical_not(jnp.logical_and(mine, sta == s)))
        def _():
            remote(
                part.at[0, pl.ds(0, 16)], got.at[s], send.at[0], recv.at[s], {"tm": source_tm, "sta": s}
            ).wait_recv()

    total = got[0]
    for s in range(1, 8):
        total = total + got[s]
    out[...] = total


ANY = pl.BlockSpec(memory_space=pl.ANY)
IN_VMEM = pl.BlockSpec(memory_space=VMEM)
IN_SMEM = pl.BlockSpec(memory_space=pltpu.SMEM)
DMA = pltpu.SemaphoreType.DMA


def shards(waveforms, templates, available, moveout, bank_blocks):
    flags = jnp.stack([available, moveout], axis=2).astype(jnp.bfloat16)
    flags = jnp.pad(flags, ((0, 0), (0, 0), (0, 0), (0, LANES - CH)))
    bank = jnp.concatenate([jnp.pad(templates, ((0, 0), (0, 0), (0, 0), (0, LANES - TLEN))), flags], axis=2)
    bf16, f32 = jnp.bfloat16, jnp.float32
    got_bank, got_wave, got_halo = pl.pallas_call(
        exchange_kernel,
        out_shape=(
            jax.ShapeDtypeStruct((4, 8, ROWS, LANES), bf16),
            jax.ShapeDtypeStruct((2, 2, CH, SEG), bf16),
            jax.ShapeDtypeStruct((2, CH, 256), bf16),
        ),
        in_specs=[IN_SMEM, ANY, ANY],
        out_specs=(IN_VMEM, IN_VMEM, IN_VMEM),
        scratch_shapes=[
            VMEM((2, 2, 32, ROWS, LANES), bf16),
            VMEM((2, 32, ROWS, LANES), bf16),
            VMEM((2, 4, 8, ROWS, LANES), bf16),
            DMA((2,)), DMA((3,)), DMA((3,)), DMA((4,)), DMA((2,)), DMA, DMA,
            DMA((7,)), DMA((7,)), DMA((3,)), DMA((3,)),
        ],
        compiler_params=pltpu.CompilerParams(collective_id=1, has_side_effects=True, vmem_limit_bytes=40 * MIB),
    )(bank_blocks, bank, waveforms)
    part = pl.pallas_call(
        correlate_kernel,
        out_shape=jax.ShapeDtypeStruct((4, 32, SEG), f32),
        in_specs=[IN_VMEM, IN_VMEM, IN_VMEM],
        out_specs=IN_VMEM,
        scratch_shapes=[
            VMEM((32 * ROWS, LANES), f32),
            VMEM((CH, 32, LANES), bf16),
            VMEM((CH, 32, LANES), jnp.int32),
            VMEM((4, ROWS, EXT), f32),
            VMEM((4, ROWS, CORR), f32),
            VMEM((4, CH, LANES, CORR), bf16),
        ],
        compiler_params=pltpu.CompilerParams(vmem_limit_bytes=56 * MIB),
    )(got_bank.reshape(32, ROWS, LANES), got_wave, got_halo)
    return pl.pallas_call(
        reduce_kernel,
        out_shape=jax.ShapeDtypeStruct((16, SEG), f32),
        in_specs=[IN_VMEM],
        out_specs=IN_VMEM,
        scratch_shapes=[VMEM((8, 16, SEG), f32), DMA((8,)), DMA((8,))],
        compiler_params=pltpu.CompilerParams(collective_id=2, has_side_effects=True),
    )(part)


def solution(mesh):
    in_specs = (
        P("sta", "tm"),
        P("tm", None, "sta", None),
        P("tm", None, "sta"),
        P("tm", None, "sta"),
        P(),
    )
    return jax.shard_map(shards, mesh=mesh, in_specs=in_specs, out_specs=P("sta", "tm"), check_vma=False)
```

```python
import jax
import jax.numpy as jnp
from jax import lax
from jax.experimental import pallas as pl
from jax.experimental.pallas import tpu as pltpu
from jax.sharding import PartitionSpec as P

TLEN = 100
EPS = 1e-06
SEG = 512
EXT = 768
CORR = 640
CH = 30
ROWS = 32
LANES = 128
HROWS = 112
CHUNKS = ((0, 15), (15, 30))
HELD = (17, 15)
MESH = pl.DeviceIdType.MESH
VMEM = pltpu.VMEM
DMA = pltpu.SemaphoreType.DMA
MIB = 1 << 20


def place():
    tm = lax.axis_index("tm")
    return tm // 8, (tm // 2) % 4, tm % 2


def at_tm(y, z, h):
    return {"tm": y * 8 + z * 2 + h}


def remote(src, dst, send, recv, device):
    return pltpu.make_async_remote_copy(
        src_ref=src, dst_ref=dst, send_sem=send, recv_sem=recv, device_id=device, device_id_type=MESH
    )


def left(x, n):
    return pltpu.roll(x, x.shape[1] - n, 1)


def window_sum(x):
    two = x + left(x, 1)
    four = two + left(two, 2)
    eight = four + left(four, 4)
    sixteen = eight + left(eight, 8)
    half = sixteen + left(sixteen, 16)
    full = half + left(half, 32)
    return full + left(half, 64) + left(four, 96)


def kernel(
    blocks, bank, avail, shift, wave, out,
    cores0, cores1, core_flags, cand0, cand1, pieces0, pieces1, got0, got1, got_wave, got_halo,
    ext, scale, hankel, unit, index, part, got_part,
    local_sem, wave_send, wave_recv, halo_send, halo_recv, core_send, core_recv,
    piece_send, piece_recv, gather_send, gather_recv, part_send, part_recv,
):
    y, z, h = place()
    tm = lax.axis_index("tm")
    sta = lax.axis_index("sta")
    flags = (avail, shift)
    cores, cand, pieces, got = (cores0, cores1), (cand0, cand1), (pieces0, pieces1), (got0, got1)
    locals_ = [
        pltpu.make_async_copy(bank.at[:, a:b, pl.ds(32 * h, 32)], cores[i].at[h], local_sem.at[i])
        for i, (a, b) in enumerate(CHUNKS)
    ]
    local_flags = [pltpu.make_async_copy(flags[f], core_flags.at[h, f], local_sem.at[2 + f]) for f in range(2)]
    local_wave = pltpu.make_async_copy(wave, got_wave.at[y, h], local_sem.at[4])
    for copy in locals_ + local_flags + [local_wave]:
        copy.start()

    source_tm = (sta // 4) * 8 + z * 2 + (sta // 2) % 2
    mine = source_tm == tm
    barrier = pltpu.get_barrier_semaphore()
    for d in range(1, 16):
        pl.semaphore_signal(barrier, inc=1, device_id={"tm": (tm + d) % 16}, device_id_type=MESH)
    for s in range(8):
        @pl.when(jnp.logical_not(jnp.logical_and(mine, sta == s)))
        def _():
            pl.semaphore_signal(barrier, inc=1, device_id={"tm": source_tm, "sta": s}, device_id_type=MESH)

    @pl.when(mine)
    def _():
        pl.semaphore_wait(barrier, 22)

    @pl.when(jnp.logical_not(mine))
    def _():
        pl.semaphore_wait(barrier, 23)

    partner = at_tm(y, z, 1 - h)
    to_flags = [
        remote(flags[f], core_flags.at[h, f], core_send.at[2 + f], core_recv.at[2 + f], partner) for f in range(2)
    ]
    to_core = [
        remote(
            bank.at[:, a:b, pl.ds(32 * (1 - h), 32)], cores[i].at[h], core_send.at[i], core_recv.at[i], partner
        )
        for i, (a, b) in enumerate(CHUNKS)
    ]
    for copy in to_flags + to_core:
        copy.start()
    waves = []
    for dy, dh in ((0, 1), (1, 0), (1, 1)):
        i = dy * 2 + dh - 1
        copy = remote(
            wave, got_wave.at[y, h], wave_send.at[i], wave_recv.at[i], at_tm((y + dy) % 2, z, (h + dh) % 2)
        )
        copy.start()
        waves.append(copy)

    run = jnp.where(z > 0, y, 1 - y)

    def halo_copy(k):
        return remote(
            wave.at[:, pl.ds(0, 256)], got_halo.at[run], halo_send.at[k], halo_recv.at[run],
            at_tm(k // 2, (z + 3) % 4, k % 2),
        )

    @pl.when(h == 0)
    def _():
        for k in range(4):
            halo_copy(k).start()

    for copy in local_flags + to_flags:
        copy.wait()
    sends = []
    for i, (a, b) in enumerate(CHUNKS):
        locals_[i].wait()
        to_core[i].wait()
        for q in range(2):
            block = blocks[q]
            core, slot = (block // 2) % 2, block % 2
            for z2 in range(4):
                cand[i][q, z2, 0 : b - a, :, 0:TLEN] = cores[i][core, slot, :, 8 * z2 : 8 * z2 + 8]
            if i == 0:
                for f in range(2):
                    both = core_flags[core, f].astype(jnp.float32)
                    rows = jnp.where(slot == 0, both[:, 0, :], both[:, 1, :]).astype(jnp.bfloat16)
                    for z2 in range(4):
                        top = min(8, CH - 8 * z2)
                        cand[i][q, z2, b - a + f, 0:top, 0:64] = rows[8 * z2 : 8 * z2 + top]
        for d in range(1, 8):
            y2, z2 = (y + d // 4) % 2, (z + d) % 4
            copy = remote(
                cand[i].at[y2, z2], pieces[i].at[y, z], piece_send.at[i, d - 1], piece_recv.at[i, d - 1],
                at_tm(y2, z2, h),
            )
            copy.start()
            sends.append((i, copy))

    local_wave.wait()
    for copy in waves:
        copy.wait()
    for r in range(2):
        remote(
            wave.at[:, pl.ds(0, 256)], got_halo.at[r], halo_send.at[0], halo_recv.at[r], at_tm(0, (z + 1) % 4, 0)
        ).wait_recv()
    for s in range(4):
        run, core = s // 2, s % 2
        ext[s, 0:CH, 0:SEG] = got_wave[run, core].astype(jnp.float32)
        if core == 0:
            tail = got_wave[run, 1, :, 0:256].astype(jnp.float32)
        else:
            tail = got_halo[run].astype(jnp.float32)
            if run == 1:
                tail = jnp.where(z == 3, jnp.zeros_like(tail), tail)
        ext[s, 0:CH, SEG:EXT] = tail

    def lags(s):
        x = ext[s]
        first = window_sum(x)[:, :CORR] * (1.0 / TLEN)
        second = window_sum(x * x)[:, :CORR] * (1.0 / TLEN)
        scale[s] = lax.rsqrt(second - first * first + EPS)

        def one(c, carry):
            wide = jnp.broadcast_to(ext[s, pl.ds(c, 1), :], (HROWS, EXT))
            turned = pltpu.roll(wide, EXT - (HROWS - 1), 1, stride=1, stride_axis=0)
            hankel[s, c, 0:HROWS, :] = turned[:, :CORR].astype(jnp.bfloat16)
            hankel[s, c, HROWS:, :] = jnp.zeros((LANES - HROWS, CORR), jnp.bfloat16)
            return carry

        lax.fori_loop(0, CH, one, 0, unroll=3)

    @pl.loop(0, 3)
    def _(s):
        lags(s)

    lane = lax.broadcasted_iota(jnp.int32, (8, LANES), 1)
    live = lane < TLEN
    flip = (HROWS - 1 - lane) & (LANES - 1)
    owner = blocks[y] // 2
    owner_y, owner_z = owner // 8, (owner // 2) % 4
    gathers = []
    for i, (a, b) in enumerate(CHUNKS):
        for k, copy in sends:
            if k == i:
                copy.wait_recv()
        here = jnp.logical_and(owner_y == y, owner_z == z)

        def kept(c):
            return jnp.where(
                here, cand[i][y, z, c].astype(jnp.float32), pieces[i][owner_y, owner_z, c].astype(jnp.float32)
            )

        def one(c, carry):
            v = kept(c)
            v = jnp.where(live, v, 0.0)
            mean = jnp.sum(v, axis=1, keepdims=True) * (1.0 / TLEN)
            dev = jnp.where(live, v - mean, 0.0)
            spread = jnp.sqrt(jnp.sum(dev * dev, axis=1, keepdims=True) * (1.0 / TLEN) + EPS)
            u = dev / (spread * TLEN)
            got[i][z, c] = jnp.take_along_axis(u, flip, axis=1).astype(jnp.bfloat16)
            return carry

        lax.fori_loop(0, b - a, one, 0, unroll=5)
        for f in range(HELD[i] - (b - a)):
            got[i][z, b - a + f] = kept(b - a + f).astype(jnp.bfloat16)
        for d in range(1, 4):
            copy = remote(
                got[i].at[z], got[i].at[z], gather_send.at[i, d - 1], gather_recv.at[i, d - 1],
                at_tm(y, (z + d) % 4, h),
            )
            copy.start()
            gathers.append((i, copy))
        if i == 0:
            lags(3)

    def sum_copy(s, j):
        y2, h2 = s // 2, s % 2
        to_tm = y2 * 8 + z * 2 + h2
        to_sta = 4 * y + 2 * h + j
        itself = jnp.logical_and(to_tm == tm, to_sta == sta)
        src = part.at[s, pl.ds(16 * j, 16)]
        k = 2 * s + j
        return itself, src, remote(
            src, got_part.at[sta], part_send.at[k], part_recv.at[sta], {"tm": to_tm, "sta": to_sta}
        )

    wide_lane = lax.broadcasted_iota(jnp.int32, (ROWS, LANES), 1)
    for i, (a, b) in enumerate(CHUNKS):
        for k, copy in gathers:
            if k == i:
                copy.wait_recv()
        if i == 0:
            tables = []
            for f in range(2):
                table = jnp.transpose(got[0][:, b - a + f].astype(jnp.float32).reshape(ROWS, LANES))
                tables.append(jnp.where(h == 0, table[0:32], table[32:64]))
        for c in range(a, b):
            w = jnp.broadcast_to(tables[0][:, c : c + 1], (ROWS, LANES))
            u = got[i][:, c - a].astype(jnp.float32).reshape(ROWS, LANES)
            unit[c] = (u * w).astype(jnp.bfloat16)
            index[c] = wide_lane + jnp.broadcast_to(tables[1][:, c : c + 1], (ROWS, LANES)).astype(jnp.int32)

        @pl.loop(0, 4)
        def _(s):
            if i == 0:
                acc = [jnp.zeros((ROWS, LANES), jnp.float32) for _ in range(4)]
            else:
                acc = [part[s, :, LANES * m : LANES * (m + 1)] for m in range(4)]
            for c in range(a, b):
                corr = jnp.dot(unit[c], hankel[s, c], preferred_element_type=jnp.float32)
                corr = corr * scale[s, pl.ds(c, 1), :]
                where = index[c]
                inside = where < LANES
                at = where & (LANES - 1)
                turned = [
                    jnp.take_along_axis(corr[:, LANES * m : LANES * (m + 1)], at, axis=1) for m in range(5)
                ]
                acc = [v + jnp.where(inside, turned[m], turned[m + 1]) for m, v in enumerate(acc)]
            for m in range(4):
                part[s, :, LANES * m : LANES * (m + 1)] = acc[m]
            if i == len(CHUNKS) - 1:
                for j in range(2):
                    itself, src, away = sum_copy(s, j)

                    @pl.when(jnp.logical_not(itself))
                    def _():
                        away.start()

                    @pl.when(itself)
                    def _():
                        got_part[sta] = src[...]

    for s in range(8):
        @pl.when(jnp.logical_not(jnp.logical_and(mine, sta == s)))
        def _():
            remote(
                part.at[0, pl.ds(0, 16)], got_part.at[s], part_send.at[0], part_recv.at[s],
                {"tm": source_tm, "sta": s},
            ).wait_recv()

    total = got_part[0]
    for s in range(1, 8):
        total = total + got_part[s]
    out[...] = total
    @pl.when(h == 0)
    def _():
        for k in range(4):
            halo_copy(k).wait_send()

    for _, copy in sends + gathers:
        copy.wait_send()
    for s in range(4):
        for j in range(2):
            itself, _, away = sum_copy(s, j)

            @pl.when(jnp.logical_not(itself))
            def _():
                away.wait_send()


ANY = pl.BlockSpec(memory_space=pl.ANY)
IN_VMEM = pl.BlockSpec(memory_space=VMEM)
IN_SMEM = pl.BlockSpec(memory_space=pltpu.SMEM)


def shards(waveforms, templates, available, moveout, bank_blocks):
    bf16, f32, i32 = jnp.bfloat16, jnp.float32, jnp.int32
    return pl.pallas_call(
        kernel,
        out_shape=jax.ShapeDtypeStruct((16, SEG), f32),
        in_specs=[IN_SMEM, ANY, ANY, ANY, ANY],
        out_specs=IN_VMEM,
        scratch_shapes=[
            *(VMEM((2, 2, b - a, 32, TLEN), bf16) for a, b in CHUNKS),
            VMEM((2, 2, CH, 2, 64), i32),
            *(VMEM((2, 4, n, 8, LANES), bf16) for n in HELD),
            *(VMEM((2, 4, n, 8, LANES), bf16) for n in HELD),
            *(VMEM((4, n, 8, LANES), bf16) for n in HELD),
            VMEM((2, 2, CH, SEG), bf16),
            VMEM((2, CH, 256), bf16),
            VMEM((4, ROWS, EXT), f32),
            VMEM((4, ROWS, CORR), f32),
            VMEM((4, CH, LANES, CORR), bf16),
            VMEM((CH, ROWS, LANES), bf16),
            VMEM((CH, ROWS, LANES), i32),
            VMEM((4, ROWS, SEG), f32),
            VMEM((8, 16, SEG), f32),
            DMA((5,)), DMA((3,)), DMA((3,)), DMA((4,)), DMA((2,)), DMA((4,)), DMA((4,)),
            DMA((2, 7)), DMA((2, 7)), DMA((2, 3)), DMA((2, 3)), DMA((8,)), DMA((8,)),
        ],
        compiler_params=pltpu.CompilerParams(collective_id=1, has_side_effects=True, vmem_limit_bytes=60 * MIB),
    )(
        bank_blocks,
        jnp.transpose(templates, (0, 2, 1, 3)),
        jnp.transpose(available, (2, 0, 1)),
        jnp.transpose(moveout, (2, 0, 1)),
        waveforms,
    )


def solution(mesh):
    in_specs = (
        P("sta", "tm"),
        P("tm", None, "sta", None),
        P("tm", None, "sta"),
        P("tm", None, "sta"),
        P(),
    )
    return jax.shard_map(shards, mesh=mesh, in_specs=in_specs, out_specs=P("sta", "tm"), check_vma=False)
```

```python
import jax
import jax.numpy as jnp
from jax import lax
from jax.experimental import pallas as pl
from jax.experimental.pallas import tpu as pltpu
from jax.sharding import PartitionSpec as P

TLEN = 100
EPS = 1e-06
SEG = 512
RUN = 1024
EXT = 1280
CORR = 1152
CH = 30
ROWS = 64
LANES = 128
HROWS = 112
CHUNKS = ((0, 15), (15, 30))
HELD = tuple(b - a + (2 if a == 0 else 0) for a, b in CHUNKS)
N = len(CHUNKS)
MESH = pl.DeviceIdType.MESH
VMEM = pltpu.VMEM
DMA = pltpu.SemaphoreType.DMA
MIB = 1 << 20


def place():
    tm = lax.axis_index("tm")
    return tm // 8, (tm // 2) % 4, tm % 2


def at_tm(y, z, h):
    return {"tm": y * 8 + z * 2 + h}


def remote(src, dst, send, recv, device):
    return pltpu.make_async_remote_copy(
        src_ref=src, dst_ref=dst, send_sem=send, recv_sem=recv, device_id=device, device_id_type=MESH
    )


def left(x, n):
    return pltpu.roll(x, x.shape[1] - n, 1)


def window_sum(x):
    two = x + left(x, 1)
    four = two + left(two, 2)
    eight = four + left(four, 4)
    sixteen = eight + left(eight, 8)
    half = sixteen + left(sixteen, 16)
    full = half + left(half, 32)
    return full + left(half, 64) + left(four, 96)


def kernel(blocks, bank, avail, shift, wave, out, *scratch):
    cores, cand, pieces, got = (scratch[k * N : k * N + N] for k in range(4))
    (
        core_flags, got_wave, got_halo, ext, scale, hankel, unit, index, part, got_part,
        local_sem, wave_send, wave_recv, halo_send, halo_recv, core_send, core_recv,
        piece_send, piece_recv, gather_send, gather_recv, part_send, part_recv,
    ) = scratch[4 * N :]
    y, z, h = place()
    tm = lax.axis_index("tm")
    sta = lax.axis_index("sta")
    flags = (avail, shift)
    locals_ = [
        pltpu.make_async_copy(bank.at[:, a:b, pl.ds(32 * h, 32)], cores[i].at[h], local_sem.at[i])
        for i, (a, b) in enumerate(CHUNKS)
    ]
    local_flags = [pltpu.make_async_copy(flags[f], core_flags.at[h, f], local_sem.at[N + f]) for f in range(2)]
    local_wave = pltpu.make_async_copy(wave, got_wave.at[h], local_sem.at[N + 2])
    for copy in local_flags + locals_ + [local_wave]:
        copy.start()

    source_h = (sta // 2) % 2
    mine = source_h == h
    source_tm = y * 8 + z * 2 + source_h
    barrier = pltpu.get_barrier_semaphore()
    for d in range(1, 16):
        pl.semaphore_signal(barrier, inc=1, device_id={"tm": (tm + d) % 16}, device_id_type=MESH)
    for s in range(8):
        @pl.when(jnp.logical_not(jnp.logical_and(mine, sta == s)))
        def _():
            pl.semaphore_signal(barrier, inc=1, device_id={"tm": source_tm, "sta": s}, device_id_type=MESH)

    @pl.when(mine)
    def _():
        pl.semaphore_wait(barrier, 22)

    @pl.when(jnp.logical_not(mine))
    def _():
        pl.semaphore_wait(barrier, 23)

    partner = at_tm(y, z, 1 - h)
    to_flags = [
        remote(flags[f], core_flags.at[h, f], core_send.at[N + f], core_recv.at[N + f], partner) for f in range(2)
    ]
    to_core = [
        remote(
            bank.at[:, a:b, pl.ds(32 * (1 - h), 32)], cores[i].at[h], core_send.at[i], core_recv.at[i], partner
        )
        for i, (a, b) in enumerate(CHUNKS)
    ]
    to_wave = remote(wave, got_wave.at[h], wave_send, wave_recv, partner)
    before_y, before_z = jnp.where(z > 0, y, 1 - y), (z + 3) % 4

    def halo_copy(k):
        return remote(wave.at[:, pl.ds(0, 256)], got_halo, halo_send.at[k], halo_recv, at_tm(before_y, before_z, k))

    for copy in to_flags + to_core[:1]:
        copy.start()

    @pl.when(h == 0)
    def _():
        for k in range(2):
            halo_copy(k).start()

    for copy in to_core[1:] + [to_wave]:
        copy.start()

    for copy in local_flags + to_flags:
        copy.wait()
    sends = []
    for i, (a, b) in enumerate(CHUNKS):
        locals_[i].wait()
        to_core[i].wait()
        for q in range(2):
            block = blocks[q]
            core, slot = (block // 2) % 2, block % 2
            for z2 in range(4):
                cand[i][q, z2, 0 : b - a, :, 0:TLEN] = cores[i][core, slot, :, 8 * z2 : 8 * z2 + 8]
            if i == 0:
                for f in range(2):
                    both = core_flags[core, f].astype(jnp.float32)
                    rows = jnp.where(slot == 0, both[:, 0, :], both[:, 1, :]).astype(jnp.bfloat16)
                    for z2 in range(4):
                        top = min(8, CH - 8 * z2)
                        cand[i][q, z2, b - a + f, 0:top, 0:64] = rows[8 * z2 : 8 * z2 + top]
        for d in range(1, 8):
            y2, z2 = (y + d // 4) % 2, (z + d) % 4
            copy = remote(
                cand[i].at[y2, z2], pieces[i].at[y, z], piece_send.at[i, d - 1], piece_recv.at[i, d - 1],
                at_tm(y2, z2, h),
            )
            copy.start()
            sends.append((i, copy))

    local_wave.wait()
    to_wave.wait()
    remote(wave.at[:, pl.ds(0, 256)], got_halo, halo_send.at[0], halo_recv, partner).wait_recv()
    for core in range(2):
        ext[0:CH, SEG * core : SEG * core + SEG] = got_wave[core].astype(jnp.float32)
    tail = got_halo[...].astype(jnp.float32)
    ext[0:CH, RUN:EXT] = jnp.where(jnp.logical_and(y == 1, z == 3), jnp.zeros_like(tail), tail)

    def lags(c, carry):
        wide = jnp.broadcast_to(ext[pl.ds(c, 1), :], (HROWS, EXT))
        turned = pltpu.roll(wide, EXT - (HROWS - 1), 1, stride=1, stride_axis=0)
        hankel[c] = turned[:, :CORR].astype(jnp.bfloat16)
        return carry

    lax.fori_loop(0, CH, lags, 0, unroll=5)
    x = ext[...]
    first = window_sum(x)[:, :CORR] * (1.0 / TLEN)
    second = window_sum(x * x)[:, :CORR] * (1.0 / TLEN)
    scale[...] = lax.rsqrt(second - first * first + EPS)

    lane = lax.broadcasted_iota(jnp.int32, (8, LANES), 1)
    live = lane < TLEN
    flip = (HROWS - 1 - lane) & (LANES - 1)
    owner = blocks[y] // 2
    owner_y, owner_z = owner // 8, (owner // 2) % 4
    here = jnp.logical_and(owner_y == y, owner_z == z)
    own = 4 * y + z
    gathers = []
    for i, (a, b) in enumerate(CHUNKS):
        for k, copy in sends:
            if k == i:
                copy.wait_recv()

        def kept(c):
            return jnp.where(
                here, cand[i][y, z, c].astype(jnp.float32), pieces[i][owner_y, owner_z, c].astype(jnp.float32)
            )

        for c in range(b - a):
            v = jnp.where(live, kept(c), 0.0)
            mean = jnp.sum(v, axis=1, keepdims=True) * (1.0 / TLEN)
            dev = jnp.where(live, v - mean, 0.0)
            spread = jnp.sqrt(jnp.sum(dev * dev, axis=1, keepdims=True) * (1.0 / TLEN) + EPS)
            u = dev / (spread * TLEN)
            got[i][own, c] = jnp.take_along_axis(u, flip, axis=1).astype(jnp.bfloat16)
        for c in range(b - a, HELD[i]):
            got[i][own, c] = kept(c).astype(jnp.bfloat16)
        for d in range(1, 8):
            copy = remote(
                got[i].at[own], got[i].at[own], gather_send.at[i, d - 1], gather_recv.at[i, d - 1],
                at_tm((y + d // 4) % 2, (z + d) % 4, h),
            )
            copy.start()
            gathers.append((i, copy))

    def sum_copy(r, h2):
        to_tm = y * 8 + z * 2 + h2
        to_sta = 4 * (r // 2) + 2 * h + r % 2
        itself = jnp.logical_and(h == h2, to_sta == sta)
        src = part.at[pl.ds(16 * r, 16), pl.ds(SEG * h2, SEG)]
        return itself, src, remote(
            src, got_part.at[sta], part_send.at[2 * r + h2], part_recv.at[sta], {"tm": to_tm, "sta": to_sta}
        )

    wide_lane = lax.broadcasted_iota(jnp.int32, (ROWS, LANES), 1)
    for i, (a, b) in enumerate(CHUNKS):
        for k, copy in gathers:
            if k == i:
                copy.wait_recv()
        if i == 0:
            tables = []
            for f in range(2):
                halves = []
                for q in range(2):
                    table = jnp.transpose(
                        got[0][4 * q : 4 * q + 4, b - a + f].astype(jnp.float32).reshape(32, LANES)
                    )
                    halves.append(jnp.where(h == 0, table[0:32], table[32:64]))
                tables.append(jnp.concatenate(halves, axis=0))
        for c in range(a, b):
            w = jnp.broadcast_to(tables[0][:, c : c + 1], (ROWS, LANES))
            u = got[i][:, c - a].astype(jnp.float32).reshape(ROWS, LANES)
            unit[c] = (u * w).astype(jnp.bfloat16)
            index[c] = wide_lane + jnp.broadcast_to(tables[1][:, c : c + 1], (ROWS, LANES)).astype(jnp.int32)
        if i == N - 1:
            for _, copy in sends:
                copy.wait_send()

            @pl.when(h == 0)
            def _():
                for k in range(2):
                    halo_copy(k).wait_send()

        @pl.loop(0, 4)
        def _(r):
            rows = pl.ds(pl.multiple_of(16 * r, 16), 16)
            if i == 0:
                acc = [jnp.zeros((16, LANES), jnp.float32) for _ in range(8)]
            else:
                acc = [part[rows, LANES * m : LANES * (m + 1)] for m in range(8)]
            for c in range(a, b):
                corr = jnp.dot(unit[c, rows, 0:HROWS], hankel[c], preferred_element_type=jnp.float32)
                corr = corr * scale[pl.ds(c, 1), :]
                where = index[c, rows, :]
                inside = where < LANES
                at = where & (LANES - 1)
                turned = [
                    jnp.take_along_axis(corr[:, LANES * m : LANES * (m + 1)], at, axis=1) for m in range(9)
                ]
                acc = [v + jnp.where(inside, turned[m], turned[m + 1]) for m, v in enumerate(acc)]
            for m in range(8):
                part[rows, LANES * m : LANES * (m + 1)] = acc[m]
            if i == N - 1:
                for h2 in range(2):
                    itself, src, away = sum_copy(r, h2)

                    @pl.when(jnp.logical_not(itself))
                    def _():
                        away.start()

                    @pl.when(itself)
                    def _():
                        got_part[sta] = src[...]

    for _, copy in gathers:
        copy.wait_send()
    for s in range(8):
        @pl.when(jnp.logical_not(jnp.logical_and(mine, sta == s)))
        def _():
            remote(
                part.at[pl.ds(0, 16), pl.ds(0, SEG)], got_part.at[s], part_send.at[0], part_recv.at[s],
                {"tm": source_tm, "sta": s},
            ).wait_recv()

    total = got_part[0]
    for s in range(1, 8):
        total = total + got_part[s]
    out[...] = total
    for r in range(4):
        for h2 in range(2):
            itself, _, away = sum_copy(r, h2)

            @pl.when(jnp.logical_not(itself))
            def _():
                away.wait_send()


ANY = pl.BlockSpec(memory_space=pl.ANY)
IN_VMEM = pl.BlockSpec(memory_space=VMEM)
IN_SMEM = pl.BlockSpec(memory_space=pltpu.SMEM)


def shards(waveforms, templates, available, moveout, bank_blocks):
    bf16, f32, i32 = jnp.bfloat16, jnp.float32, jnp.int32
    return pl.pallas_call(
        kernel,
        out_shape=jax.ShapeDtypeStruct((16, SEG), f32),
        in_specs=[IN_SMEM, ANY, ANY, ANY, ANY],
        out_specs=IN_VMEM,
        scratch_shapes=[
            *(VMEM((2, 2, b - a, 32, TLEN), bf16) for a, b in CHUNKS),
            *(VMEM((2, 4, n, 8, LANES), bf16) for n in HELD),
            *(VMEM((2, 4, n, 8, LANES), bf16) for n in HELD),
            *(VMEM((8, n, 8, LANES), bf16) for n in HELD),
            VMEM((2, 2, CH, 2, 64), i32),
            VMEM((2, CH, SEG), bf16),
            VMEM((CH, 256), bf16),
            VMEM((32, EXT), f32),
            VMEM((32, CORR), f32),
            VMEM((CH, HROWS, CORR), bf16),
            VMEM((CH, ROWS, LANES), bf16),
            VMEM((CH, ROWS, LANES), i32),
            VMEM((ROWS, RUN), f32),
            VMEM((8, 16, SEG), f32),
            DMA((N + 3,)), DMA, DMA, DMA((2,)), DMA, DMA((N + 2,)), DMA((N + 2,)),
            DMA((N, 7)), DMA((N, 7)), DMA((N, 7)), DMA((N, 7)), DMA((8,)), DMA((8,)),
        ],
        compiler_params=pltpu.CompilerParams(collective_id=1, has_side_effects=True, vmem_limit_bytes=60 * MIB),
    )(
        bank_blocks,
        jnp.transpose(templates, (0, 2, 1, 3)),
        jnp.transpose(available, (2, 0, 1)),
        jnp.transpose(moveout, (2, 0, 1)),
        waveforms,
    )


def solution(mesh):
    in_specs = (
        P("sta", "tm"),
        P("tm", None, "sta", None),
        P("tm", None, "sta"),
        P("tm", None, "sta"),
        P(),
    )
    return jax.shard_map(shards, mesh=mesh, in_specs=in_specs, out_specs=P("sta", "tm"), check_vma=False)
```

```python
import jax
import jax.numpy as jnp
from jax import lax
from jax.experimental import pallas as pl
from jax.experimental.pallas import tpu as pltpu
from jax.sharding import PartitionSpec as P

TLEN = 100
EPS = 1e-06
SEG = 512
RUN = 1024
EXT = 1280
CORR = 1152
CH = 30
ROWS = 64
LANES = 128
HROWS = 112
CHUNKS = ((0, 15), (15, 30))
HELD = tuple(b - a + (2 if a == 0 else 0) for a, b in CHUNKS)
N = len(CHUNKS)
MESH = pl.DeviceIdType.MESH
VMEM = pltpu.VMEM
DMA = pltpu.SemaphoreType.DMA
MIB = 1 << 20


def place():
    tm = lax.axis_index("tm")
    return tm // 8, (tm // 2) % 4, tm % 2


def at_tm(y, z, h):
    return {"tm": y * 8 + z * 2 + h}


def remote(src, dst, send, recv, device):
    return pltpu.make_async_remote_copy(
        src_ref=src, dst_ref=dst, send_sem=send, recv_sem=recv, device_id=device, device_id_type=MESH
    )


def left(x, n):
    return pltpu.roll(x, x.shape[1] - n, 1)


def window_sum(x):
    two = x + left(x, 1)
    four = two + left(two, 2)
    eight = four + left(four, 4)
    sixteen = eight + left(eight, 8)
    half = sixteen + left(sixteen, 16)
    full = half + left(half, 32)
    return full + left(half, 64) + left(four, 96)


def kernel(which, bank, avail, shift, wave, out, *scratch):
    cores, cand, pieces, got = (scratch[k * N : k * N + N] for k in range(4))
    (
        blocks, core_flags, got_wave, got_halo, ext, scale, hankel, unit, index, part, got_part,
        local_sem, wave_send, wave_recv, halo_send, halo_recv, core_send, core_recv,
        piece_send, piece_recv, gather_send, gather_recv, part_send, part_recv,
    ) = scratch[4 * N :]
    y, z, h = place()
    tm = lax.axis_index("tm")
    sta = lax.axis_index("sta")
    flags = (avail, shift)
    locals_ = [
        pltpu.make_async_copy(bank.at[:, a:b, pl.ds(32 * h, 32)], cores[i].at[h], local_sem.at[i])
        for i, (a, b) in enumerate(CHUNKS)
    ]
    local_flags = [pltpu.make_async_copy(flags[f], core_flags.at[h, f], local_sem.at[N + f]) for f in range(2)]
    local_wave = pltpu.make_async_copy(wave, got_wave.at[h], local_sem.at[N + 2])
    local_blocks = pltpu.make_async_copy(which, blocks, local_sem.at[N + 3])
    for copy in [local_blocks] + local_flags + locals_ + [local_wave]:
        copy.start()

    source_h = (sta // 2) % 2
    mine = source_h == h
    source_tm = y * 8 + z * 2 + source_h
    barrier = pltpu.get_barrier_semaphore()
    partner = at_tm(y, z, 1 - h)
    for d in range(1, 8):
        pl.semaphore_signal(barrier, inc=1, device_id=at_tm((y + d // 4) % 2, (z + d) % 4, h), device_id_type=MESH)
    pl.semaphore_signal(barrier, inc=1, device_id=partner, device_id_type=MESH)
    after = at_tm(jnp.where(z < 3, y, 1 - y), (z + 1) % 4, 0)

    @pl.when(h == 1)
    def _():
        pl.semaphore_signal(barrier, inc=1, device_id=after, device_id_type=MESH)

    for s in range(8):
        @pl.when(jnp.logical_not(jnp.logical_and(mine, sta == s)))
        def _():
            pl.semaphore_signal(barrier, inc=1, device_id={"tm": source_tm, "sta": s}, device_id_type=MESH)

    for first in range(2):
        for both in range(2):
            @pl.when(jnp.logical_and(h == first, mine if both else jnp.logical_not(mine)))
            def _():
                pl.semaphore_wait(barrier, 17 - first - both)

    to_flags = [
        remote(flags[f], core_flags.at[h, f], core_send.at[N + f], core_recv.at[N + f], partner) for f in range(2)
    ]
    to_core = [
        remote(
            bank.at[:, a:b, pl.ds(32 * (1 - h), 32)], cores[i].at[h], core_send.at[i], core_recv.at[i], partner
        )
        for i, (a, b) in enumerate(CHUNKS)
    ]
    to_wave = remote(wave, got_wave.at[h], wave_send, wave_recv, partner)
    before_y, before_z = jnp.where(z > 0, y, 1 - y), (z + 3) % 4

    def halo_copy(k):
        return remote(wave.at[:, pl.ds(0, 256)], got_halo, halo_send.at[k], halo_recv, at_tm(before_y, before_z, k))

    for copy in to_flags + to_core[:1]:
        copy.start()

    @pl.when(h == 0)
    def _():
        for k in range(2):
            halo_copy(k).start()

    for copy in to_core[1:] + [to_wave]:
        copy.start()

    for copy in [local_blocks] + local_flags + to_flags:
        copy.wait()
    sends = []
    for i, (a, b) in enumerate(CHUNKS):
        locals_[i].wait()
        to_core[i].wait()
        for q in range(2):
            block = blocks[q]
            core, slot = (block // 2) % 2, block % 2
            for z2 in range(4):
                cand[i][q, z2, 0 : b - a, :, 0:TLEN] = cores[i][core, slot, :, 8 * z2 : 8 * z2 + 8]
            if i == 0:
                for f in range(2):
                    both = core_flags[core, f].astype(jnp.float32)
                    rows = jnp.where(slot == 0, both[:, 0, :], both[:, 1, :]).astype(jnp.bfloat16)
                    for z2 in range(4):
                        top = min(8, CH - 8 * z2)
                        cand[i][q, z2, b - a + f, 0:top, 0:64] = rows[8 * z2 : 8 * z2 + top]
        for d in range(1, 8):
            y2, z2 = (y + d // 4) % 2, (z + d) % 4
            copy = remote(
                cand[i].at[y2, z2], pieces[i].at[y, z], piece_send.at[i, d - 1], piece_recv.at[i, d - 1],
                at_tm(y2, z2, h),
            )
            copy.start()
            sends.append((i, copy))

    local_wave.wait()
    to_wave.wait()
    remote(wave.at[:, pl.ds(0, 256)], got_halo, halo_send.at[0], halo_recv, partner).wait_recv()
    for core in range(2):
        ext[0:CH, SEG * core : SEG * core + SEG] = got_wave[core].astype(jnp.float32)
    tail = got_halo[...].astype(jnp.float32)
    ext[0:CH, RUN:EXT] = jnp.where(jnp.logical_and(y == 1, z == 3), jnp.zeros_like(tail), tail)

    def lags(c, carry):
        wide = jnp.broadcast_to(ext[pl.ds(c, 1), :], (HROWS, EXT))
        turned = pltpu.roll(wide, EXT - (HROWS - 1), 1, stride=1, stride_axis=0)
        hankel[c] = turned[:, :CORR].astype(jnp.bfloat16)
        return carry

    lax.fori_loop(0, CH, lags, 0, unroll=5)
    x = ext[...]
    first = window_sum(x)[:, :CORR] * (1.0 / TLEN)
    second = window_sum(x * x)[:, :CORR] * (1.0 / TLEN)
    scale[...] = lax.rsqrt(second - first * first + EPS)

    lane = lax.broadcasted_iota(jnp.int32, (8, LANES), 1)
    live = lane < TLEN
    flip = (HROWS - 1 - lane) & (LANES - 1)
    owner = blocks[y] // 2
    owner_y, owner_z = owner // 8, (owner // 2) % 4
    here = jnp.logical_and(owner_y == y, owner_z == z)
    own = 4 * y + z
    gathers = []
    for i, (a, b) in enumerate(CHUNKS):
        for k, copy in sends:
            if k == i:
                copy.wait_recv()

        def kept(c):
            return jnp.where(
                here, cand[i][y, z, c].astype(jnp.float32), pieces[i][owner_y, owner_z, c].astype(jnp.float32)
            )

        for c in range(b - a):
            v = jnp.where(live, kept(c), 0.0)
            mean = jnp.sum(v, axis=1, keepdims=True) * (1.0 / TLEN)
            dev = jnp.where(live, v - mean, 0.0)
            spread = jnp.sqrt(jnp.sum(dev * dev, axis=1, keepdims=True) * (1.0 / TLEN) + EPS)
            u = dev / (spread * TLEN)
            got[i][own, c] = jnp.take_along_axis(u, flip, axis=1).astype(jnp.bfloat16)
        for c in range(b - a, HELD[i]):
            got[i][own, c] = kept(c).astype(jnp.bfloat16)
        for d in range(1, 8):
            copy = remote(
                got[i].at[own], got[i].at[own], gather_send.at[i, d - 1], gather_recv.at[i, d - 1],
                at_tm((y + d // 4) % 2, (z + d) % 4, h),
            )
            copy.start()
            gathers.append((i, copy))

    def sum_copy(r, h2):
        to_tm = y * 8 + z * 2 + h2
        to_sta = 4 * (r // 2) + 2 * h + r % 2
        itself = jnp.logical_and(h == h2, to_sta == sta)
        src = part.at[pl.ds(16 * r, 16), pl.ds(SEG * h2, SEG)]
        return itself, src, remote(
            src, got_part.at[sta], part_send.at[2 * r + h2], part_recv.at[sta], {"tm": to_tm, "sta": to_sta}
        )

    wide_lane = lax.broadcasted_iota(jnp.int32, (ROWS, LANES), 1)
    for i, (a, b) in enumerate(CHUNKS):
        for k, copy in gathers:
            if k == i:
                copy.wait_recv()
        if i == 0:
            tables = []
            for f in range(2):
                halves = []
                for q in range(2):
                    table = jnp.transpose(
                        got[0][4 * q : 4 * q + 4, b - a + f].astype(jnp.float32).reshape(32, LANES)
                    )
                    halves.append(jnp.where(h == 0, table[0:32], table[32:64]))
                tables.append(jnp.concatenate(halves, axis=0))
        for c in range(a, b):
            w = jnp.broadcast_to(tables[0][:, c : c + 1], (ROWS, LANES))
            u = got[i][:, c - a].astype(jnp.float32).reshape(ROWS, LANES)
            unit[c] = (u * w).astype(jnp.bfloat16)
            index[c] = wide_lane + jnp.broadcast_to(tables[1][:, c : c + 1], (ROWS, LANES)).astype(jnp.int32)
        if i == N - 1:
            for _, copy in sends:
                copy.wait_send()

            @pl.when(h == 0)
            def _():
                for k in range(2):
                    halo_copy(k).wait_send()

        @pl.loop(0, 4)
        def _(r):
            rows = pl.ds(pl.multiple_of(16 * r, 16), 16)
            if i == 0:
                acc = [jnp.zeros((16, LANES), jnp.float32) for _ in range(8)]
            else:
                acc = [part[rows, LANES * m : LANES * (m + 1)] for m in range(8)]
            for c in range(a, b):
                corr = jnp.dot(unit[c, rows, 0:HROWS], hankel[c], preferred_element_type=jnp.float32)
                corr = corr * scale[pl.ds(c, 1), :]
                where = index[c, rows, :]
                inside = where < LANES
                at = where & (LANES - 1)
                turned = [
                    jnp.take_along_axis(corr[:, LANES * m : LANES * (m + 1)], at, axis=1) for m in range(9)
                ]
                acc = [v + jnp.where(inside, turned[m], turned[m + 1]) for m, v in enumerate(acc)]
            for m in range(8):
                part[rows, LANES * m : LANES * (m + 1)] = acc[m]
            if i == N - 1:
                for h2 in range(2):
                    itself, src, away = sum_copy(r, h2)

                    @pl.when(jnp.logical_not(itself))
                    def _():
                        away.start()

                    @pl.when(itself)
                    def _():
                        got_part[sta] = src[...]

    for _, copy in gathers:
        copy.wait_send()
    for s in range(8):
        @pl.when(jnp.logical_not(jnp.logical_and(mine, sta == s)))
        def _():
            remote(
                part.at[pl.ds(0, 16), pl.ds(0, SEG)], got_part.at[s], part_send.at[0], part_recv.at[s],
                {"tm": source_tm, "sta": s},
            ).wait_recv()

    total = got_part[0]
    for s in range(1, 8):
        total = total + got_part[s]
    out[...] = total
    for r in range(4):
        for h2 in range(2):
            itself, _, away = sum_copy(r, h2)

            @pl.when(jnp.logical_not(itself))
            def _():
                away.wait_send()


ANY = pl.BlockSpec(memory_space=pltpu.HBM)
IN_VMEM = pl.BlockSpec(memory_space=VMEM)


def shards(waveforms, templates, available, moveout, bank_blocks):
    bf16, f32, i32 = jnp.bfloat16, jnp.float32, jnp.int32
    return pl.pallas_call(
        kernel,
        out_shape=jax.ShapeDtypeStruct((16, SEG), f32),
        in_specs=[ANY, ANY, ANY, ANY, ANY],
        out_specs=IN_VMEM,
        scratch_shapes=[
            *(VMEM((2, 2, b - a, 32, TLEN), bf16) for a, b in CHUNKS),
            *(VMEM((2, 4, n, 8, LANES), bf16) for n in HELD),
            *(VMEM((2, 4, n, 8, LANES), bf16) for n in HELD),
            *(VMEM((8, n, 8, LANES), bf16) for n in HELD),
            pltpu.SMEM((2,), i32),
            VMEM((2, 2, CH, 2, 64), i32),
            VMEM((2, CH, SEG), bf16),
            VMEM((CH, 256), bf16),
            VMEM((32, EXT), f32),
            VMEM((32, CORR), f32),
            VMEM((CH, HROWS, CORR), bf16),
            VMEM((CH, ROWS, LANES), bf16),
            VMEM((CH, ROWS, LANES), i32),
            VMEM((ROWS, RUN), f32),
            VMEM((8, 16, SEG), f32),
            DMA((N + 4,)), DMA, DMA, DMA((2,)), DMA, DMA((N + 2,)), DMA((N + 2,)),
            DMA((N, 7)), DMA((N, 7)), DMA((N, 7)), DMA((N, 7)), DMA((8,)), DMA((8,)),
        ],
        compiler_params=pltpu.CompilerParams(collective_id=1, has_side_effects=True, vmem_limit_bytes=32 * MIB),
    )(
        pltpu.with_memory_space_constraint(bank_blocks, pltpu.HBM),
        pltpu.with_memory_space_constraint(jnp.transpose(templates, (0, 2, 1, 3)), pltpu.HBM),
        pltpu.with_memory_space_constraint(jnp.transpose(available, (2, 0, 1)), pltpu.HBM),
        pltpu.with_memory_space_constraint(jnp.transpose(moveout, (2, 0, 1)), pltpu.HBM),
        pltpu.with_memory_space_constraint(waveforms, pltpu.HBM),
    )


def solution(mesh):
    in_specs = (
        P("sta", "tm"),
        P("tm", None, "sta", None),
        P("tm", None, "sta"),
        P("tm", None, "sta"),
        P(),
    )
    return jax.shard_map(shards, mesh=mesh, in_specs=in_specs, out_specs=P("sta", "tm"), check_vma=False)
```

```python
import jax
import jax.numpy as jnp
from jax import lax
from jax.experimental import pallas as pl
from jax.experimental.pallas import tpu as pltpu
from jax.sharding import PartitionSpec as P

TLEN = 100
EPS = 1e-06
SEG = 512
RUN = 1024
EXT = 1280
CORR = 1152
CH = 30
ROWS = 64
LANES = 128
HROWS = 112
CHUNKS = ((0, 15), (15, 30))
N = len(CHUNKS)
HOSTS, GUESTS, QUARTER = 12, 3, 25
HELD = (HOSTS + 1, HOSTS)
FAR_FIRST = (6, 5, 7, 4, 2, 1, 3)
MESH = pl.DeviceIdType.MESH
VMEM = pltpu.VMEM
DMA = pltpu.SemaphoreType.DMA
MIB = 1 << 20


def place():
    tm = lax.axis_index("tm")
    return tm // 8, (tm // 2) % 4, tm % 2


def at_tm(y, z, h):
    return {"tm": y * 8 + z * 2 + h}


def remote(src, dst, send, recv, device):
    return pltpu.make_async_remote_copy(
        src_ref=src, dst_ref=dst, send_sem=send, recv_sem=recv, device_id=device, device_id_type=MESH
    )


def left(x, n):
    return pltpu.roll(x, x.shape[1] - n, 1)


def guest(tiles, lane):
    out = pltpu.roll(tiles[0], LANES - TLEN, 1)
    for p in range(1, 4):
        out = jnp.where(lane >= QUARTER * p, pltpu.roll(tiles[p], LANES - TLEN + QUARTER * p, 1), out)
    return out


def window_sum(x):
    two = x + left(x, 1)
    four = two + left(two, 2)
    eight = four + left(four, 4)
    sixteen = eight + left(eight, 8)
    half = sixteen + left(sixteen, 16)
    full = half + left(half, 32)
    return full + left(half, 64) + left(four, 96)


def kernel(which, bank, avail, shift, wave, out, *scratch):
    cores, cand, pieces, got = (scratch[k * N : k * N + N] for k in range(4))
    (
        blocks, staging, late, core_flags, got_wave, got_halo, ext, scale, hankel, unit, index, part, got_part,
        local_sem, wave_send, wave_recv, halo_send, halo_recv, core_send, core_recv,
        piece_send, piece_recv, gather_send, gather_recv, part_send, part_recv,
    ) = scratch[4 * N :]
    y, z, h = place()
    tm = lax.axis_index("tm")
    sta = lax.axis_index("sta")
    flags = (avail, shift)
    locals_ = [
        pltpu.make_async_copy(bank.at[:, a:b, pl.ds(32 * h, 32)], cores[i].at[h], local_sem.at[i])
        for i, (a, b) in enumerate(CHUNKS)
    ]
    local_flags = [pltpu.make_async_copy(flags[f], core_flags.at[h, f], local_sem.at[N + f]) for f in range(2)]
    local_wave = pltpu.make_async_copy(wave, got_wave.at[h], local_sem.at[N + 2])
    local_blocks = pltpu.make_async_copy(which, blocks, local_sem.at[N + 3])
    for copy in [local_blocks] + local_flags + locals_ + [local_wave]:
        copy.start()

    source_h = (sta // 2) % 2
    mine = source_h == h
    source_tm = y * 8 + z * 2 + source_h
    barrier = pltpu.get_barrier_semaphore()
    partner = at_tm(y, z, 1 - h)
    for d in range(1, 8):
        pl.semaphore_signal(barrier, inc=1, device_id=at_tm((y + d // 4) % 2, (z + d) % 4, h), device_id_type=MESH)
    pl.semaphore_signal(barrier, inc=1, device_id=partner, device_id_type=MESH)
    after = at_tm(jnp.where(z < 3, y, 1 - y), (z + 1) % 4, 0)

    @pl.when(h == 1)
    def _():
        pl.semaphore_signal(barrier, inc=1, device_id=after, device_id_type=MESH)

    for s in range(8):
        @pl.when(jnp.logical_not(jnp.logical_and(mine, sta == s)))
        def _():
            pl.semaphore_signal(barrier, inc=1, device_id={"tm": source_tm, "sta": s}, device_id_type=MESH)

    for first in range(2):
        for both in range(2):
            @pl.when(jnp.logical_and(h == first, mine if both else jnp.logical_not(mine)))
            def _():
                pl.semaphore_wait(barrier, 17 - first - both)

    to_flags = [
        remote(flags[f], core_flags.at[h, f], core_send.at[N + f], core_recv.at[N + f], partner) for f in range(2)
    ]
    to_core = [
        remote(
            bank.at[:, a:b, pl.ds(32 * (1 - h), 32)], cores[i].at[h], core_send.at[i], core_recv.at[i], partner
        )
        for i, (a, b) in enumerate(CHUNKS)
    ]
    to_wave = remote(wave, got_wave.at[h], wave_send, wave_recv, partner)
    before_y, before_z = jnp.where(z > 0, y, 1 - y), (z + 3) % 4

    def halo_copy(k):
        return remote(wave.at[:, pl.ds(0, 256)], got_halo, halo_send.at[k], halo_recv, at_tm(before_y, before_z, k))

    for copy in to_flags + to_core[:1]:
        copy.start()

    @pl.when(h == 0)
    def _():
        for k in range(2):
            halo_copy(k).start()

    for copy in to_core[1:] + [to_wave]:
        copy.start()

    for copy in [local_blocks] + local_flags + to_flags:
        copy.wait()
    sends = []
    for i, (a, b) in enumerate(CHUNKS):
        locals_[i].wait()
        to_core[i].wait()
        for q in range(2):
            block = blocks[q]
            core, slot = (block // 2) % 2, block % 2
            for z2 in range(4):
                cand[i][q, z2, 0:HOSTS, :, 0:TLEN] = cores[i][core, slot, 0:HOSTS, 8 * z2 : 8 * z2 + 8]
            staging[q, :, :, 0:TLEN] = cores[i][core, slot, HOSTS:].astype(jnp.float32)
            for k in range(HOSTS):
                moved = pltpu.roll(staging[q, k // 4], TLEN - QUARTER * (k % 4), 1)
                for z2 in range(4):
                    cand[i][q, z2, k, :, TLEN : TLEN + QUARTER] = moved[
                        8 * z2 : 8 * z2 + 8, TLEN : TLEN + QUARTER
                    ].astype(jnp.bfloat16)
            if i == 0:
                rows = []
                for f in range(2):
                    both = core_flags[core, f].astype(jnp.float32)
                    rows.append(jnp.where(slot == 0, both[:, 0, :], both[:, 1, :]))
                rows = jnp.concatenate(rows, axis=1).astype(jnp.bfloat16)
                for z2 in range(4):
                    top = min(8, CH - 8 * z2)
                    cand[i][q, z2, HOSTS, 0:top] = rows[8 * z2 : 8 * z2 + top]
        for d in FAR_FIRST:
            y2, z2 = (y + d // 4) % 2, (z + d) % 4
            copy = remote(
                cand[i].at[y2, z2], pieces[i].at[y, z], piece_send.at[i, d - 1], piece_recv.at[i, d - 1],
                at_tm(y2, z2, h),
            )
            copy.start()
            sends.append((i, copy))

    local_wave.wait()
    to_wave.wait()
    remote(wave.at[:, pl.ds(0, 256)], got_halo, halo_send.at[0], halo_recv, partner).wait_recv()
    for core in range(2):
        ext[0:CH, SEG * core : SEG * core + SEG] = got_wave[core].astype(jnp.float32)
    tail = got_halo[...].astype(jnp.float32)
    ext[0:CH, RUN:EXT] = jnp.where(jnp.logical_and(y == 1, z == 3), jnp.zeros_like(tail), tail)

    late[...] = pltpu.roll(ext[...], HROWS - TLEN, 1)

    def lags(c, carry):
        wide = jnp.broadcast_to(late[pl.ds(c, 1), :], (HROWS, EXT))
        turned = pltpu.roll(wide, EXT - (HROWS - 1), 1, stride=1, stride_axis=0)
        hankel[c] = turned[:, :CORR].astype(jnp.bfloat16)
        return carry

    lax.fori_loop(*CHUNKS[0], lags, 0, unroll=5)

    lane = lax.broadcasted_iota(jnp.int32, (8, LANES), 1)
    live = lane < TLEN
    flip = (TLEN - 1 - lane) & (LANES - 1)
    owner = blocks[y] // 2
    owner_y, owner_z = owner // 8, (owner // 2) % 4
    here = jnp.logical_and(owner_y == y, owner_z == z)
    own = 4 * y + z
    gathers = []
    for i, (a, b) in enumerate(CHUNKS):
        for k, copy in sends:
            if k == i:
                copy.wait_recv()

        def kept(c):
            return jnp.where(
                here, cand[i][y, z, c].astype(jnp.float32), pieces[i][owner_y, owner_z, c].astype(jnp.float32)
            )

        tiles = [kept(k) for k in range(HOSTS)]
        units = []
        for v in tiles + [guest(tiles[4 * g : 4 * g + 4], lane) for g in range(GUESTS)]:
            v = jnp.where(live, v, 0.0)
            mean = jnp.sum(v, axis=1, keepdims=True) * (1.0 / TLEN)
            dev = jnp.where(live, v - mean, 0.0)
            spread = jnp.sqrt(jnp.sum(dev * dev, axis=1, keepdims=True) * (1.0 / TLEN) + EPS)
            u = dev / (spread * TLEN)
            units.append(jnp.take_along_axis(u, flip, axis=1))
        for k in range(HOSTS):
            moved = pltpu.roll(units[HOSTS + k // 4], TLEN - QUARTER * (k % 4), 1)
            got[i][own, k] = jnp.where(live, units[k], moved).astype(jnp.bfloat16)
        if i == 0:
            got[i][own, HOSTS] = kept(HOSTS).astype(jnp.bfloat16)
        for d in FAR_FIRST:
            copy = remote(
                got[i].at[own], got[i].at[own], gather_send.at[i, d - 1], gather_recv.at[i, d - 1],
                at_tm((y + d // 4) % 2, (z + d) % 4, h),
            )
            copy.start()
            gathers.append((i, copy))
        if i == 0:
            lax.fori_loop(*CHUNKS[1], lags, 0, unroll=5)

    x = ext[...]
    first = window_sum(x)[:, :CORR] * (1.0 / TLEN)
    second = window_sum(x * x)[:, :CORR] * (1.0 / TLEN)
    scale[...] = lax.rsqrt(second - first * first + EPS)

    def sum_copy(r, h2):
        to_tm = y * 8 + z * 2 + h2
        to_sta = 4 * (r // 2) + 2 * h + r % 2
        itself = jnp.logical_and(h == h2, to_sta == sta)
        src = part.at[pl.ds(16 * r, 16), pl.ds(SEG * h2, SEG)]
        return itself, src, remote(
            src, got_part.at[sta], part_send.at[2 * r + h2], part_recv.at[sta], {"tm": to_tm, "sta": to_sta}
        )

    wide_lane = lax.broadcasted_iota(jnp.int32, (ROWS, LANES), 1)
    for i, (a, b) in enumerate(CHUNKS):
        for k, copy in gathers:
            if k == i:
                copy.wait_recv()
        if i == 0:
            halves = ([], [])
            for q in range(2):
                table = jnp.transpose(got[0][4 * q : 4 * q + 4, HOSTS].astype(jnp.float32).reshape(32, LANES))
                for f in range(2):
                    halves[f].append(jnp.where(h == 0, table[64 * f : 64 * f + 32], table[64 * f + 32 : 64 * f + 64]))
            tables = [jnp.concatenate(half, axis=0) for half in halves]
        tiles = [got[i][:, k].astype(jnp.float32).reshape(ROWS, LANES) for k in range(HOSTS)]
        tiles = tiles + [guest(tiles[4 * g : 4 * g + 4], wide_lane) for g in range(GUESTS)]
        for c in range(a, b):
            w = jnp.broadcast_to(tables[0][:, c : c + 1], (ROWS, LANES))
            unit[c] = jnp.where(wide_lane < TLEN, tiles[c - a] * w, 0.0).astype(jnp.bfloat16)
            index[c] = wide_lane + jnp.broadcast_to(tables[1][:, c : c + 1], (ROWS, LANES)).astype(jnp.int32)
        if i == N - 1:
            for _, copy in sends:
                copy.wait_send()

            @pl.when(h == 0)
            def _():
                for k in range(2):
                    halo_copy(k).wait_send()

        @pl.loop(0, 4)
        def _(r):
            rows = pl.ds(pl.multiple_of(16 * r, 16), 16)
            if i == 0:
                acc = [jnp.zeros((16, LANES), jnp.float32) for _ in range(8)]
            else:
                acc = [part[rows, LANES * m : LANES * (m + 1)] for m in range(8)]
            for c in range(a, b):
                corr = jnp.dot(unit[c, rows, 0:HROWS], hankel[c], preferred_element_type=jnp.float32)
                corr = corr * scale[pl.ds(c, 1), :]
                where = index[c, rows, :]
                inside = where < LANES
                at = where & (LANES - 1)
                turned = [
                    jnp.take_along_axis(corr[:, LANES * m : LANES * (m + 1)], at, axis=1) for m in range(9)
                ]
                acc = [v + jnp.where(inside, turned[m], turned[m + 1]) for m, v in enumerate(acc)]
            for m in range(8):
                part[rows, LANES * m : LANES * (m + 1)] = acc[m]
            if i == N - 1:
                for h2 in range(2):
                    itself, src, away = sum_copy(r, h2)

                    @pl.when(jnp.logical_not(itself))
                    def _():
                        away.start()

                    @pl.when(itself)
                    def _():
                        got_part[sta] = src[...]

    for _, copy in gathers:
        copy.wait_send()
    for s in range(8):
        @pl.when(jnp.logical_not(jnp.logical_and(mine, sta == s)))
        def _():
            remote(
                part.at[pl.ds(0, 16), pl.ds(0, SEG)], got_part.at[s], part_send.at[0], part_recv.at[s],
                {"tm": source_tm, "sta": s},
            ).wait_recv()

    total = got_part[0]
    for s in range(1, 8):
        total = total + got_part[s]
    out[...] = total
    for r in range(4):
        for h2 in range(2):
            itself, _, away = sum_copy(r, h2)

            @pl.when(jnp.logical_not(itself))
            def _():
                away.wait_send()


ANY = pl.BlockSpec(memory_space=pltpu.HBM)
IN_VMEM = pl.BlockSpec(memory_space=VMEM)


def shards(waveforms, templates, available, moveout, bank_blocks):
    bf16, f32, i32 = jnp.bfloat16, jnp.float32, jnp.int32
    return pl.pallas_call(
        kernel,
        out_shape=jax.ShapeDtypeStruct((16, SEG), f32),
        in_specs=[ANY, ANY, ANY, ANY, ANY],
        out_specs=IN_VMEM,
        scratch_shapes=[
            *(VMEM((2, 2, b - a, 32, TLEN), bf16) for a, b in CHUNKS),
            *(VMEM((2, 4, n, 8, LANES), bf16) for n in HELD),
            *(VMEM((2, 4, n, 8, LANES), bf16) for n in HELD),
            *(VMEM((8, n, 8, LANES), bf16) for n in HELD),
            pltpu.SMEM((2,), i32),
            VMEM((2, GUESTS, 32, LANES), f32),
            VMEM((32, EXT), f32),
            VMEM((2, 2, CH, 2, 64), i32),
            VMEM((2, CH, SEG), bf16),
            VMEM((CH, 256), bf16),
            VMEM((32, EXT), f32),
            VMEM((32, CORR), f32),
            VMEM((CH, HROWS, CORR), bf16),
            VMEM((CH, ROWS, LANES), bf16),
            VMEM((CH, ROWS, LANES), i32),
            VMEM((ROWS, RUN), f32),
            VMEM((8, 16, SEG), f32),
            DMA((N + 4,)), DMA, DMA, DMA((2,)), DMA, DMA((N + 2,)), DMA((N + 2,)),
            DMA((N, 7)), DMA((N, 7)), DMA((N, 7)), DMA((N, 7)), DMA((8,)), DMA((8,)),
        ],
        compiler_params=pltpu.CompilerParams(collective_id=1, has_side_effects=True, vmem_limit_bytes=32 * MIB),
    )(
        pltpu.with_memory_space_constraint(bank_blocks, pltpu.HBM),
        pltpu.with_memory_space_constraint(jnp.transpose(templates, (0, 2, 1, 3)), pltpu.HBM),
        pltpu.with_memory_space_constraint(jnp.transpose(available, (2, 0, 1)), pltpu.HBM),
        pltpu.with_memory_space_constraint(jnp.transpose(moveout, (2, 0, 1)), pltpu.HBM),
        pltpu.with_memory_space_constraint(waveforms, pltpu.HBM),
    )


def solution(mesh):
    in_specs = (
        P("sta", "tm"),
        P("tm", None, "sta", None),
        P("tm", None, "sta"),
        P("tm", None, "sta"),
        P(),
    )
    return jax.shard_map(shards, mesh=mesh, in_specs=in_specs, out_specs=P("sta", "tm"), check_vma=False)
```

```python
import jax
import jax.numpy as jnp
from jax import lax
from jax.experimental import pallas as pl
from jax.experimental.pallas import tpu as pltpu
from jax.sharding import PartitionSpec as P

TLEN = 100
EPS = 1e-06
SEG = 512
RUN = 1024
EXT = 1280
CORR = 1152
CH = 30
ROWS = 64
LANES = 128
HROWS = 112
CHUNKS = ((0, 15), (15, 30))
N = len(CHUNKS)
HOSTS, GUESTS, QUARTER = 12, 3, 25
HELD = (HOSTS + 1, HOSTS)
UNUSED = 512.0
FAR_FIRST = (6, 5, 7, 4, 2, 1, 3)
MESH = pl.DeviceIdType.MESH
VMEM = pltpu.VMEM
DMA = pltpu.SemaphoreType.DMA
MIB = 1 << 20


def place():
    tm = lax.axis_index("tm")
    return tm // 8, (tm // 2) % 4, tm % 2


def at_tm(y, z, h):
    return {"tm": y * 8 + z * 2 + h}


def remote(src, dst, send, recv, device):
    return pltpu.make_async_remote_copy(
        src_ref=src, dst_ref=dst, send_sem=send, recv_sem=recv, device_id=device, device_id_type=MESH
    )


def left(x, n):
    return pltpu.roll(x, x.shape[1] - n, 1)


def guest(tiles, lane):
    out = pltpu.roll(tiles[0], LANES - TLEN, 1)
    for p in range(1, 4):
        out = jnp.where(lane >= QUARTER * p, pltpu.roll(tiles[p], LANES - TLEN + QUARTER * p, 1), out)
    return out


def window_sum(x):
    two = x + left(x, 1)
    four = two + left(two, 2)
    eight = four + left(four, 4)
    sixteen = eight + left(eight, 8)
    half = sixteen + left(sixteen, 16)
    full = half + left(half, 32)
    return full + left(half, 64) + left(four, 96)


def kernel(which, bank, avail, shift, wave, out, *scratch):
    cores, cand, pieces, got = (scratch[k * N : k * N + N] for k in range(4))
    (
        blocks, staging, late, core_flags, got_wave, got_halo, ext, scale, hankel, unit, index, part, got_part,
        local_sem, wave_send, wave_recv, halo_send, halo_recv, core_send, core_recv,
        piece_send, piece_recv, gather_send, gather_recv, part_send, part_recv,
    ) = scratch[4 * N :]
    y, z, h = place()
    tm = lax.axis_index("tm")
    sta = lax.axis_index("sta")
    flags = (avail, shift)
    locals_ = [
        pltpu.make_async_copy(bank.at[:, a:b, pl.ds(32 * h, 32)], cores[i].at[h], local_sem.at[i])
        for i, (a, b) in enumerate(CHUNKS)
    ]
    local_flags = [pltpu.make_async_copy(flags[f], core_flags.at[h, f], local_sem.at[N + f]) for f in range(2)]
    local_wave = pltpu.make_async_copy(wave, got_wave.at[h], local_sem.at[N + 2])
    local_blocks = pltpu.make_async_copy(which, blocks, local_sem.at[N + 3])
    for copy in [local_blocks] + local_flags + locals_ + [local_wave]:
        copy.start()

    source_h = (sta // 2) % 2
    mine = source_h == h
    source_tm = y * 8 + z * 2 + source_h
    barrier = pltpu.get_barrier_semaphore()
    partner = at_tm(y, z, 1 - h)
    for d in range(1, 8):
        pl.semaphore_signal(barrier, inc=1, device_id=at_tm((y + d // 4) % 2, (z + d) % 4, h), device_id_type=MESH)
    pl.semaphore_signal(barrier, inc=1, device_id=partner, device_id_type=MESH)
    after = at_tm(jnp.where(z < 3, y, 1 - y), (z + 1) % 4, 0)

    @pl.when(h == 1)
    def _():
        pl.semaphore_signal(barrier, inc=1, device_id=after, device_id_type=MESH)

    for s in range(8):
        @pl.when(jnp.logical_not(jnp.logical_and(mine, sta == s)))
        def _():
            pl.semaphore_signal(barrier, inc=1, device_id={"tm": source_tm, "sta": s}, device_id_type=MESH)

    for first in range(2):
        for both in range(2):
            @pl.when(jnp.logical_and(h == first, mine if both else jnp.logical_not(mine)))
            def _():
                pl.semaphore_wait(barrier, 17 - first - both)

    to_flags = [
        remote(flags[f], core_flags.at[h, f], core_send.at[N + f], core_recv.at[N + f], partner) for f in range(2)
    ]
    to_core = [
        remote(
            bank.at[:, a:b, pl.ds(32 * (1 - h), 32)], cores[i].at[h], core_send.at[i], core_recv.at[i], partner
        )
        for i, (a, b) in enumerate(CHUNKS)
    ]
    to_wave = remote(wave, got_wave.at[h], wave_send, wave_recv, partner)
    before_y, before_z = jnp.where(z > 0, y, 1 - y), (z + 3) % 4

    def halo_copy(k):
        return remote(wave.at[:, pl.ds(0, 256)], got_halo, halo_send.at[k], halo_recv, at_tm(before_y, before_z, k))

    for copy in to_flags + to_core[:1]:
        copy.start()

    @pl.when(h == 0)
    def _():
        for k in range(2):
            halo_copy(k).start()

    for copy in to_core[1:] + [to_wave]:
        copy.start()

    for copy in [local_blocks] + local_flags + to_flags:
        copy.wait()
    sends = []
    for i, (a, b) in enumerate(CHUNKS):
        locals_[i].wait()
        to_core[i].wait()
        for q in range(2):
            block = blocks[q]
            core, slot = (block // 2) % 2, block % 2
            for z2 in range(4):
                cand[i][q, z2, 0:HOSTS, :, 0:TLEN] = cores[i][core, slot, 0:HOSTS, 8 * z2 : 8 * z2 + 8]
            staging[q, :, :, 0:TLEN] = cores[i][core, slot, HOSTS:].astype(jnp.float32)
            for k in range(HOSTS):
                moved = pltpu.roll(staging[q, k // 4], TLEN - QUARTER * (k % 4), 1)
                for z2 in range(4):
                    cand[i][q, z2, k, :, TLEN : TLEN + QUARTER] = moved[
                        8 * z2 : 8 * z2 + 8, TLEN : TLEN + QUARTER
                    ].astype(jnp.bfloat16)
            if i == 0:
                rows = []
                for f in range(2):
                    both = core_flags[core, f].astype(jnp.float32)
                    rows.append(jnp.where(slot == 0, both[:, 0, :], both[:, 1, :]))
                rows = jnp.concatenate(rows, axis=1).astype(jnp.bfloat16)
                for z2 in range(4):
                    top = min(8, CH - 8 * z2)
                    cand[i][q, z2, HOSTS, 0:top] = rows[8 * z2 : 8 * z2 + top]
        for d in FAR_FIRST:
            y2, z2 = (y + d // 4) % 2, (z + d) % 4
            copy = remote(
                cand[i].at[y2, z2], pieces[i].at[y, z], piece_send.at[i, d - 1], piece_recv.at[i, d - 1],
                at_tm(y2, z2, h),
            )
            copy.start()
            sends.append((i, copy))

    local_wave.wait()
    to_wave.wait()
    remote(wave.at[:, pl.ds(0, 256)], got_halo, halo_send.at[0], halo_recv, partner).wait_recv()
    for core in range(2):
        ext[0:CH, SEG * core : SEG * core + SEG] = got_wave[core].astype(jnp.float32)
    tail = got_halo[...].astype(jnp.float32)
    ext[0:CH, RUN:EXT] = jnp.where(jnp.logical_and(y == 1, z == 3), jnp.zeros_like(tail), tail)

    late[...] = pltpu.roll(ext[...], HROWS - TLEN, 1)

    def lags(c, carry):
        wide = jnp.broadcast_to(late[pl.ds(c, 1), :], (HROWS, EXT))
        turned = pltpu.roll(wide, EXT - (HROWS - 1), 1, stride=1, stride_axis=0)
        hankel[c] = turned[:, :CORR].astype(jnp.bfloat16)
        return carry

    lax.fori_loop(*CHUNKS[0], lags, 0, unroll=5)

    lane = lax.broadcasted_iota(jnp.int32, (8, LANES), 1)
    live = lane < TLEN
    flip = (TLEN - 1 - lane) & (LANES - 1)
    owner = blocks[y] // 2
    owner_y, owner_z = owner // 8, (owner // 2) % 4
    here = jnp.logical_and(owner_y == y, owner_z == z)
    own = 4 * y + z
    gathers = []
    for i, (a, b) in enumerate(CHUNKS):
        for k, copy in sends:
            if k == i:
                copy.wait_recv()

        def kept(c):
            return jnp.where(
                here, cand[i][y, z, c].astype(jnp.float32), pieces[i][owner_y, owner_z, c].astype(jnp.float32)
            )

        tiles = [kept(k) for k in range(HOSTS)]
        units = []
        for v in tiles + [guest(tiles[4 * g : 4 * g + 4], lane) for g in range(GUESTS)]:
            v = jnp.where(live, v, 0.0)
            mean = jnp.sum(v, axis=1, keepdims=True) * (1.0 / TLEN)
            dev = jnp.where(live, v - mean, 0.0)
            spread = jnp.sqrt(jnp.sum(dev * dev, axis=1, keepdims=True) * (1.0 / TLEN) + EPS)
            u = dev / (spread * TLEN)
            units.append(jnp.take_along_axis(u, flip, axis=1))
        for k in range(HOSTS):
            moved = pltpu.roll(units[HOSTS + k // 4], TLEN - QUARTER * (k % 4), 1)
            got[i][own, k] = jnp.where(live, units[k], moved).astype(jnp.bfloat16)
        if i == 0:
            got[i][own, HOSTS] = kept(HOSTS).astype(jnp.bfloat16)
        for d in FAR_FIRST:
            copy = remote(
                got[i].at[own], got[i].at[own], gather_send.at[i, d - 1], gather_recv.at[i, d - 1],
                at_tm((y + d // 4) % 2, (z + d) % 4, h),
            )
            copy.start()
            gathers.append((i, copy))
        if i == 0:
            lax.fori_loop(*CHUNKS[1], lags, 0, unroll=5)

    x = ext[...]
    first = window_sum(x)[:, :CORR] * (1.0 / TLEN)
    second = window_sum(x * x)[:, :CORR] * (1.0 / TLEN)
    scale[...] = lax.rsqrt(second - first * first + EPS)

    def sum_copy(r, h2):
        to_tm = y * 8 + z * 2 + h2
        to_sta = 4 * (r // 2) + 2 * h + r % 2
        itself = jnp.logical_and(h == h2, to_sta == sta)
        src = part.at[pl.ds(16 * r, 16), pl.ds(SEG * h2, SEG)]
        return itself, src, remote(
            src, got_part.at[sta], part_send.at[2 * r + h2], part_recv.at[sta], {"tm": to_tm, "sta": to_sta}
        )

    wide_lane = lax.broadcasted_iota(jnp.int32, (ROWS, LANES), 1)
    for i, (a, b) in enumerate(CHUNKS):
        for k, copy in gathers:
            if k == i:
                copy.wait_recv()
        if i == 0:
            halves = ([], [])
            for q in range(2):
                table = jnp.transpose(got[0][4 * q : 4 * q + 4, HOSTS].astype(jnp.float32).reshape(32, LANES))
                for f in range(2):
                    halves[f].append(jnp.where(h == 0, table[64 * f : 64 * f + 32], table[64 * f + 32 : 64 * f + 64]))
            used, moved = [jnp.concatenate(half, axis=0) for half in halves]
            table = jnp.where(used > 0.5, moved, UNUSED)
        tiles = [got[i][:, k].astype(jnp.float32).reshape(ROWS, LANES) for k in range(HOSTS)]
        tiles = tiles + [guest(tiles[4 * g : 4 * g + 4], wide_lane) for g in range(GUESTS)]
        for c in range(a, b):
            to = jnp.broadcast_to(table[:, c : c + 1], (ROWS, LANES))
            keep = jnp.logical_and(wide_lane < TLEN, to < UNUSED)
            unit[c] = jnp.where(keep, tiles[c - a], 0.0).astype(jnp.bfloat16)
            index[c] = wide_lane + to.astype(jnp.int32)
        @pl.loop(0, 4)
        def _(r):
            rows = pl.ds(pl.multiple_of(16 * r, 16), 16)
            if i == 0:
                acc = [jnp.zeros((16, LANES), jnp.float32) for _ in range(8)]
            else:
                acc = [part[rows, LANES * m : LANES * (m + 1)] for m in range(8)]
            for c in range(a, b):
                corr = jnp.dot(unit[c, rows, 0:HROWS], hankel[c], preferred_element_type=jnp.float32)
                corr = corr * scale[pl.ds(c, 1), :]
                where = index[c, rows, :]
                inside = where < LANES
                at = where & (LANES - 1)
                turned = [
                    jnp.take_along_axis(corr[:, LANES * m : LANES * (m + 1)], at, axis=1) for m in range(9)
                ]
                acc = [v + jnp.where(inside, turned[m], turned[m + 1]) for m, v in enumerate(acc)]
            for m in range(8):
                part[rows, LANES * m : LANES * (m + 1)] = acc[m]
            if i == N - 1:
                for h2 in range(2):
                    itself, src, away = sum_copy(r, h2)

                    @pl.when(jnp.logical_not(itself))
                    def _():
                        away.start()

                    @pl.when(itself)
                    def _():
                        got_part[sta] = src[...]

    for _, copy in sends + gathers:
        copy.wait_send()

    @pl.when(h == 0)
    def _():
        for k in range(2):
            halo_copy(k).wait_send()

    for s in range(8):
        @pl.when(jnp.logical_not(jnp.logical_and(mine, sta == s)))
        def _():
            remote(
                part.at[pl.ds(0, 16), pl.ds(0, SEG)], got_part.at[s], part_send.at[0], part_recv.at[s],
                {"tm": source_tm, "sta": s},
            ).wait_recv()

    total = got_part[0]
    for s in range(1, 8):
        total = total + got_part[s]
    out[...] = total
    for r in range(4):
        for h2 in range(2):
            itself, _, away = sum_copy(r, h2)

            @pl.when(jnp.logical_not(itself))
            def _():
                away.wait_send()


ANY = pl.BlockSpec(memory_space=pltpu.HBM)
IN_VMEM = pl.BlockSpec(memory_space=VMEM)


def shards(waveforms, templates, available, moveout, bank_blocks):
    bf16, f32, i32 = jnp.bfloat16, jnp.float32, jnp.int32
    return pl.pallas_call(
        kernel,
        out_shape=jax.ShapeDtypeStruct((16, SEG), f32),
        in_specs=[ANY, ANY, ANY, ANY, ANY],
        out_specs=IN_VMEM,
        scratch_shapes=[
            *(VMEM((2, 2, b - a, 32, TLEN), bf16) for a, b in CHUNKS),
            *(VMEM((2, 4, n, 8, LANES), bf16) for n in HELD),
            *(VMEM((2, 4, n, 8, LANES), bf16) for n in HELD),
            *(VMEM((8, n, 8, LANES), bf16) for n in HELD),
            pltpu.SMEM((2,), i32),
            VMEM((2, GUESTS, 32, LANES), f32),
            VMEM((32, EXT), f32),
            VMEM((2, 2, CH, 2, 64), i32),
            VMEM((2, CH, SEG), bf16),
            VMEM((CH, 256), bf16),
            VMEM((32, EXT), f32),
            VMEM((32, CORR), f32),
            VMEM((CH, HROWS, CORR), bf16),
            VMEM((CH, ROWS, LANES), bf16),
            VMEM((CH, ROWS, LANES), i32),
            VMEM((ROWS, RUN), f32),
            VMEM((8, 16, SEG), f32),
            DMA((N + 4,)), DMA, DMA, DMA((2,)), DMA, DMA((N + 2,)), DMA((N + 2,)),
            DMA((N, 7)), DMA((N, 7)), DMA((N, 7)), DMA((N, 7)), DMA((8,)), DMA((8,)),
        ],
        compiler_params=pltpu.CompilerParams(collective_id=1, has_side_effects=True, vmem_limit_bytes=32 * MIB),
    )(
        pltpu.with_memory_space_constraint(bank_blocks, pltpu.HBM),
        pltpu.with_memory_space_constraint(jnp.transpose(templates, (0, 2, 1, 3)), pltpu.HBM),
        pltpu.with_memory_space_constraint(jnp.transpose(available, (2, 0, 1)), pltpu.HBM),
        pltpu.with_memory_space_constraint(jnp.transpose(moveout, (2, 0, 1)), pltpu.HBM),
        pltpu.with_memory_space_constraint(waveforms, pltpu.HBM),
    )


def solution(mesh):
    in_specs = (
        P("sta", "tm"),
        P("tm", None, "sta", None),
        P("tm", None, "sta"),
        P("tm", None, "sta"),
        P(),
    )
    return jax.shard_map(shards, mesh=mesh, in_specs=in_specs, out_specs=P("sta", "tm"), check_vma=False)
```

```python
import jax
import jax.numpy as jnp
from jax import lax
from jax.experimental import pallas as pl
from jax.experimental.pallas import tpu as pltpu
from jax.sharding import PartitionSpec as P

TLEN = 100
EPS = 1e-06
SEG = 512
RUN = 1024
EXT = 1280
CORR = 1152
CH = 30
ROWS = 64
LANES = 128
HROWS = 112
CHUNKS = ((0, 15), (15, 30))
N = len(CHUNKS)
HOSTS, GUESTS, QUARTER = 12, 3, 25
HELD = (HOSTS + 1, HOSTS)
UNUSED = 512.0
FAR_FIRST = (6, 5, 7, 4, 2, 1, 3)
MESH = pl.DeviceIdType.MESH
VMEM = pltpu.VMEM
DMA = pltpu.SemaphoreType.DMA
MIB = 1 << 20


def place():
    tm = lax.axis_index("tm")
    return tm // 8, (tm // 2) % 4, tm % 2


def at_tm(y, z, h):
    return {"tm": y * 8 + z * 2 + h}


def remote(src, dst, send, recv, device):
    return pltpu.make_async_remote_copy(
        src_ref=src, dst_ref=dst, send_sem=send, recv_sem=recv, device_id=device, device_id_type=MESH
    )


def left(x, n):
    return pltpu.roll(x, x.shape[1] - n, 1)


def guest(tiles, lane):
    out = pltpu.roll(tiles[0], LANES - TLEN, 1)
    for p in range(1, 4):
        out = jnp.where(lane >= QUARTER * p, pltpu.roll(tiles[p], LANES - TLEN + QUARTER * p, 1), out)
    return out


def window_sum(x):
    two = x + left(x, 1)
    four = two + left(two, 2)
    eight = four + left(four, 4)
    sixteen = eight + left(eight, 8)
    half = sixteen + left(sixteen, 16)
    full = half + left(half, 32)
    return full + left(half, 64) + left(four, 96)


def kernel(which, bank, avail, shift, wave, out, *scratch):
    cores, cand, pieces, got = (scratch[k * N : k * N + N] for k in range(4))
    (
        blocks, staging, late, core_flags, got_wave, got_halo, ext, scale, hankel, unit, index, part, got_part,
        local_sem, wave_send, wave_recv, halo_send, halo_recv, core_send, core_recv,
        piece_send, piece_recv, gather_send, gather_recv, part_send, part_recv,
    ) = scratch[4 * N :]
    y, z, h = place()
    tm = lax.axis_index("tm")
    sta = lax.axis_index("sta")
    flags = (avail, shift)
    locals_ = [
        pltpu.make_async_copy(bank.at[:, a:b, pl.ds(32 * h, 32)], cores[i].at[h], local_sem.at[i])
        for i, (a, b) in enumerate(CHUNKS)
    ]
    local_flags = [pltpu.make_async_copy(flags[f], core_flags.at[h, f], local_sem.at[N + f]) for f in range(2)]
    local_wave = pltpu.make_async_copy(wave, got_wave.at[h], local_sem.at[N + 2])
    local_blocks = pltpu.make_async_copy(which, blocks, local_sem.at[N + 3])
    for copy in [local_blocks] + local_flags + locals_ + [local_wave]:
        copy.start()

    source_h = (sta // 2) % 2
    mine = source_h == h
    source_tm = y * 8 + z * 2 + source_h
    barrier = pltpu.get_barrier_semaphore()
    partner = at_tm(y, z, 1 - h)
    for d in range(1, 8):
        pl.semaphore_signal(barrier, inc=1, device_id=at_tm((y + d // 4) % 2, (z + d) % 4, h), device_id_type=MESH)
    pl.semaphore_signal(barrier, inc=1, device_id=partner, device_id_type=MESH)
    after = at_tm(jnp.where(z < 3, y, 1 - y), (z + 1) % 4, 0)

    @pl.when(h == 1)
    def _():
        pl.semaphore_signal(barrier, inc=1, device_id=after, device_id_type=MESH)

    for s in range(8):
        @pl.when(jnp.logical_not(jnp.logical_and(mine, sta == s)))
        def _():
            pl.semaphore_signal(barrier, inc=1, device_id={"tm": source_tm, "sta": s}, device_id_type=MESH)

    for first in range(2):
        for both in range(2):
            @pl.when(jnp.logical_and(h == first, mine if both else jnp.logical_not(mine)))
            def _():
                pl.semaphore_wait(barrier, 17 - first - both)

    to_flags = [
        remote(flags[f], core_flags.at[h, f], core_send.at[N + f], core_recv.at[N + f], partner) for f in range(2)
    ]
    to_core = [
        remote(
            bank.at[:, a:b, pl.ds(32 * (1 - h), 32)], cores[i].at[h], core_send.at[i], core_recv.at[i], partner
        )
        for i, (a, b) in enumerate(CHUNKS)
    ]
    to_wave = remote(wave, got_wave.at[h], wave_send, wave_recv, partner)
    before_y, before_z = jnp.where(z > 0, y, 1 - y), (z + 3) % 4

    def halo_copy(k):
        return remote(wave.at[:, pl.ds(0, 256)], got_halo, halo_send.at[k], halo_recv, at_tm(before_y, before_z, k))

    for copy in to_flags + to_core[:1]:
        copy.start()

    @pl.when(h == 0)
    def _():
        for k in range(2):
            halo_copy(k).start()

    for copy in to_core[1:] + [to_wave]:
        copy.start()

    for copy in [local_blocks] + local_flags + to_flags:
        copy.wait()
    sends = []
    for i, (a, b) in enumerate(CHUNKS):
        locals_[i].wait()
        to_core[i].wait()
        for away in (1, 0):
            q = (y + away) % 2
            block = blocks[q]
            core, slot = (block // 2) % 2, block % 2
            for z2 in range(4):
                cand[i][q, z2, 0:HOSTS, :, 0:TLEN] = cores[i][core, slot, 0:HOSTS, 8 * z2 : 8 * z2 + 8]
            staging[q, :, :, 0:TLEN] = cores[i][core, slot, HOSTS:].astype(jnp.float32)
            for k in range(HOSTS):
                moved = pltpu.roll(staging[q, k // 4], TLEN - QUARTER * (k % 4), 1)
                for z2 in range(4):
                    cand[i][q, z2, k, :, TLEN : TLEN + QUARTER] = moved[
                        8 * z2 : 8 * z2 + 8, TLEN : TLEN + QUARTER
                    ].astype(jnp.bfloat16)
            if i == 0:
                rows = []
                for f in range(2):
                    both = core_flags[core, f].astype(jnp.float32)
                    rows.append(jnp.where(slot == 0, both[:, 0, :], both[:, 1, :]))
                rows = jnp.concatenate(rows, axis=1).astype(jnp.bfloat16)
                for z2 in range(4):
                    top = min(8, CH - 8 * z2)
                    cand[i][q, z2, HOSTS, 0:top] = rows[8 * z2 : 8 * z2 + top]
            for d in FAR_FIRST[:4] if away else FAR_FIRST[4:]:
                z2 = (z + d) % 4
                copy = remote(
                    cand[i].at[q, z2], pieces[i].at[y, z], piece_send.at[i, d - 1], piece_recv.at[i, d - 1],
                    at_tm(q, z2, h),
                )
                copy.start()
                sends.append((i, copy))

    local_wave.wait()
    to_wave.wait()
    remote(wave.at[:, pl.ds(0, 256)], got_halo, halo_send.at[0], halo_recv, partner).wait_recv()
    for core in range(2):
        ext[0:CH, SEG * core : SEG * core + SEG] = got_wave[core].astype(jnp.float32)
    tail = got_halo[...].astype(jnp.float32)
    ext[0:CH, RUN:EXT] = jnp.where(jnp.logical_and(y == 1, z == 3), jnp.zeros_like(tail), tail)

    late[...] = pltpu.roll(ext[...], HROWS - TLEN, 1)

    def lags(c, carry):
        wide = jnp.broadcast_to(late[pl.ds(c, 1), :], (HROWS, EXT))
        turned = pltpu.roll(wide, EXT - (HROWS - 1), 1, stride=1, stride_axis=0)
        hankel[c] = turned[:, :CORR].astype(jnp.bfloat16)
        return carry

    lax.fori_loop(*CHUNKS[0], lags, 0, unroll=5)

    lane = lax.broadcasted_iota(jnp.int32, (8, LANES), 1)
    live = lane < TLEN
    flip = (TLEN - 1 - lane) & (LANES - 1)
    owner = blocks[y] // 2
    owner_y, owner_z = owner // 8, (owner // 2) % 4
    here = jnp.logical_and(owner_y == y, owner_z == z)
    own = 4 * y + z
    gathers = []
    for i, (a, b) in enumerate(CHUNKS):
        for k, copy in sends:
            if k == i:
                copy.wait_recv()

        def kept(c):
            return jnp.where(
                here, cand[i][y, z, c].astype(jnp.float32), pieces[i][owner_y, owner_z, c].astype(jnp.float32)
            )

        tiles = [kept(k) for k in range(HOSTS)]
        units = []
        for v in tiles + [guest(tiles[4 * g : 4 * g + 4], lane) for g in range(GUESTS)]:
            v = jnp.where(live, v, 0.0)
            mean = jnp.sum(v, axis=1, keepdims=True) * (1.0 / TLEN)
            dev = jnp.where(live, v - mean, 0.0)
            spread = jnp.sqrt(jnp.sum(dev * dev, axis=1, keepdims=True) * (1.0 / TLEN) + EPS)
            u = dev / (spread * TLEN)
            units.append(jnp.take_along_axis(u, flip, axis=1))
        for k in range(HOSTS):
            moved = pltpu.roll(units[HOSTS + k // 4], TLEN - QUARTER * (k % 4), 1)
            got[i][own, k] = jnp.where(live, units[k], moved).astype(jnp.bfloat16)
        if i == 0:
            got[i][own, HOSTS] = kept(HOSTS).astype(jnp.bfloat16)
        for d in FAR_FIRST:
            copy = remote(
                got[i].at[own], got[i].at[own], gather_send.at[i, d - 1], gather_recv.at[i, d - 1],
                at_tm((y + d // 4) % 2, (z + d) % 4, h),
            )
            copy.start()
            gathers.append((i, copy))
        if i == 0:
            lax.fori_loop(*CHUNKS[1], lags, 0, unroll=5)

    x = ext[...]
    first = window_sum(x)[:, :CORR] * (1.0 / TLEN)
    second = window_sum(x * x)[:, :CORR] * (1.0 / TLEN)
    scale[...] = lax.rsqrt(second - first * first + EPS)

    def sum_copy(r, h2):
        to_tm = y * 8 + z * 2 + h2
        to_sta = 4 * (r // 2) + 2 * h + r % 2
        itself = jnp.logical_and(h == h2, to_sta == sta)
        src = part.at[pl.ds(16 * r, 16), pl.ds(SEG * h2, SEG)]
        return itself, src, remote(
            src, got_part.at[sta], part_send.at[2 * r + h2], part_recv.at[sta], {"tm": to_tm, "sta": to_sta}
        )

    wide_lane = lax.broadcasted_iota(jnp.int32, (ROWS, LANES), 1)
    for i, (a, b) in enumerate(CHUNKS):
        for k, copy in gathers:
            if k == i:
                copy.wait_recv()
        if i == 0:
            halves = ([], [])
            for q in range(2):
                table = jnp.transpose(got[0][4 * q : 4 * q + 4, HOSTS].astype(jnp.float32).reshape(32, LANES))
                for f in range(2):
                    halves[f].append(jnp.where(h == 0, table[64 * f : 64 * f + 32], table[64 * f + 32 : 64 * f + 64]))
            used, moved = [jnp.concatenate(half, axis=0) for half in halves]
            table = jnp.where(used > 0.5, moved, UNUSED)
        tiles = [got[i][:, k].astype(jnp.float32).reshape(ROWS, LANES) for k in range(HOSTS)]
        tiles = tiles + [guest(tiles[4 * g : 4 * g + 4], wide_lane) for g in range(GUESTS)]
        for c in range(a, b):
            to = jnp.broadcast_to(table[:, c : c + 1], (ROWS, LANES))
            keep = jnp.logical_and(wide_lane < TLEN, to < UNUSED)
            unit[c] = jnp.where(keep, tiles[c - a], 0.0).astype(jnp.bfloat16)
            index[c] = wide_lane + to.astype(jnp.int32)
        @pl.loop(0, 4)
        def _(r):
            rows = pl.ds(pl.multiple_of(16 * r, 16), 16)
            if i == 0:
                acc = [jnp.zeros((16, LANES), jnp.float32) for _ in range(8)]
            else:
                acc = [part[rows, LANES * m : LANES * (m + 1)] for m in range(8)]
            for c in range(a, b):
                corr = jnp.dot(unit[c, rows, 0:HROWS], hankel[c], preferred_element_type=jnp.float32)
                corr = corr * scale[pl.ds(c, 1), :]
                where = index[c, rows, :]
                inside = where < LANES
                at = where & (LANES - 1)
                turned = [
                    jnp.take_along_axis(corr[:, LANES * m : LANES * (m + 1)], at, axis=1) for m in range(9)
                ]
                acc = [v + jnp.where(inside, turned[m], turned[m + 1]) for m, v in enumerate(acc)]
            for m in range(8):
                part[rows, LANES * m : LANES * (m + 1)] = acc[m]
            if i == N - 1:
                for h2 in range(2):
                    itself, src, away = sum_copy(r, h2)

                    @pl.when(jnp.logical_not(itself))
                    def _():
                        away.start()

                    @pl.when(itself)
                    def _():
                        got_part[sta] = src[...]

    for _, copy in sends + gathers:
        copy.wait_send()

    @pl.when(h == 0)
    def _():
        for k in range(2):
            halo_copy(k).wait_send()

    for s in range(8):
        @pl.when(jnp.logical_not(jnp.logical_and(mine, sta == s)))
        def _():
            remote(
                part.at[pl.ds(0, 16), pl.ds(0, SEG)], got_part.at[s], part_send.at[0], part_recv.at[s],
                {"tm": source_tm, "sta": s},
            ).wait_recv()

    total = got_part[0]
    for s in range(1, 8):
        total = total + got_part[s]
    out[...] = total
    for r in range(4):
        for h2 in range(2):
            itself, _, away = sum_copy(r, h2)

            @pl.when(jnp.logical_not(itself))
            def _():
                away.wait_send()


ANY = pl.BlockSpec(memory_space=pltpu.HBM)
IN_VMEM = pl.BlockSpec(memory_space=VMEM)


def shards(waveforms, templates, available, moveout, bank_blocks):
    bf16, f32, i32 = jnp.bfloat16, jnp.float32, jnp.int32
    return pl.pallas_call(
        kernel,
        out_shape=jax.ShapeDtypeStruct((16, SEG), f32),
        in_specs=[ANY, ANY, ANY, ANY, ANY],
        out_specs=IN_VMEM,
        scratch_shapes=[
            *(VMEM((2, 2, b - a, 32, TLEN), bf16) for a, b in CHUNKS),
            *(VMEM((2, 4, n, 8, LANES), bf16) for n in HELD),
            *(VMEM((2, 4, n, 8, LANES), bf16) for n in HELD),
            *(VMEM((8, n, 8, LANES), bf16) for n in HELD),
            pltpu.SMEM((2,), i32),
            VMEM((2, GUESTS, 32, LANES), f32),
            VMEM((32, EXT), f32),
            VMEM((2, 2, CH, 2, 64), i32),
            VMEM((2, CH, SEG), bf16),
            VMEM((CH, 256), bf16),
            VMEM((32, EXT), f32),
            VMEM((32, CORR), f32),
            VMEM((CH, HROWS, CORR), bf16),
            VMEM((CH, ROWS, LANES), bf16),
            VMEM((CH, ROWS, LANES), i32),
            VMEM((ROWS, RUN), f32),
            VMEM((8, 16, SEG), f32),
            DMA((N + 4,)), DMA, DMA, DMA((2,)), DMA, DMA((N + 2,)), DMA((N + 2,)),
            DMA((N, 7)), DMA((N, 7)), DMA((N, 7)), DMA((N, 7)), DMA((8,)), DMA((8,)),
        ],
        compiler_params=pltpu.CompilerParams(collective_id=1, has_side_effects=True, vmem_limit_bytes=32 * MIB),
    )(
        pltpu.with_memory_space_constraint(bank_blocks, pltpu.HBM),
        pltpu.with_memory_space_constraint(jnp.transpose(templates, (0, 2, 1, 3)), pltpu.HBM),
        pltpu.with_memory_space_constraint(jnp.transpose(available, (2, 0, 1)), pltpu.HBM),
        pltpu.with_memory_space_constraint(jnp.transpose(moveout, (2, 0, 1)), pltpu.HBM),
        pltpu.with_memory_space_constraint(waveforms, pltpu.HBM),
    )


def solution(mesh):
    in_specs = (
        P("sta", "tm"),
        P("tm", None, "sta", None),
        P("tm", None, "sta"),
        P("tm", None, "sta"),
        P(),
    )
    return jax.shard_map(shards, mesh=mesh, in_specs=in_specs, out_specs=P("sta", "tm"), check_vma=False)
```
